128 devices in a mesh: row: 4 (over y), col: 32 (over z, x, core).
Axes of the slice: x: 4, y: 4, z: 4, core: 2. Of those that a mesh axis runs over, the one named last changes fastest.
Arguments:
- src_cent: float32 [16, 4096], P(None, 'row'), may hold values from -6.5 to 6.5
- tgt_cent: float32 [16, 4096], P(None, 'col'), may hold values from -6.5 to 6.5
- src_mass: float32 [4096], P('row'), may hold values from 6.1035156e-05 to 0.0009765625
- tgt_mass: float32 [4096], P('col'), may hold values from 6.1035156e-05 to 0.0009765625
- src_pts: float32 [16, 262144], P(None, ('row', 'col')), may hold values from -6.5 to 6.5
- tgt_pts: float32 [16, 1048576], P(None, ('row', 'col')), may hold values from -6.5 to 6.5
- src_cluster: int32 [262144], P(('row', 'col')), may hold values from 0 to 4095
- tgt_cluster: int32 [1048576], P(('row', 'col')), may hold values from 0 to 4095
- support: int32 [1024, 16], P(('row', 'col')), may hold values from 0 to 4095, as said below
Outputs:
- coarse_f: float32 [4096], P('row')
- coarse_g: float32 [4096], P('col')
- fine_f: float32 [262144], P(('row', 'col'))
- fine_g: float32 [1048576], P(('row', 'col'))
The draws below stay inside these ranges and needn't reach their ends.
Inputs may be any that keep to these rules, and one draw needn't show every extreme that they name: `support`: each row names 16 different target blocks; every target block is named by some row; among the rows of one device (aligned blocks of 8 rows) at most 2 entries fall in any one range k * 32 to (k + 1) * 32 - 1, and exactly 2 in some such range for every device.
All inputs are finite; a program needn't handle non-finite values.
Results may differ from the reference program's by a relative error of at most 0.0003.
Values sent between devices are 32-bit elements; how exact they have to be, the bound alone decides.
A program may use at most 64 MiB of HBM per device.

```python
import math
import jax
import jax.numpy as jnp
from jax import lax

F = 16
BLK = 256
SUPP = 16
ITERS = 8
SB_DEV = 8
TB_DEV = 32
KS = 4096
KT = 4096
NS = 262144
NT = 1048576
DEVICES = 128


def point_cloud(key, rows, cols):
    first = jax.random.fold_in(key, 0)
    base = jnp.clip(jax.random.normal(first, (rows, cols), jnp.float32), -6.0, 6.0)
    return 0.25 * base


def draw_src_cent(key, part):
    return point_cloud(jax.random.fold_in(key, 101), F, KS)


def draw_tgt_cent(key, part):
    return point_cloud(jax.random.fold_in(key, 202), F, KT)


def draw_src_pts(key, part):
    return point_cloud(jax.random.fold_in(key, 303), F, NS)


def draw_tgt_pts(key, part):
    return point_cloud(jax.random.fold_in(key, 404), F, NT)


def draw_support(key, part):
    base_key = jax.random.fold_in(key, 707)
    key_shift, key_score, key_local = jax.random.split(base_key, 3)
    requests_each = SB_DEV * SUPP
    per_owner = requests_each // DEVICES
    slots_each = per_owner + 1
    device_ids = jnp.arange(DEVICES, dtype=jnp.int32)
    offset = jax.random.randint(key_shift, (), 0, DEVICES, dtype=jnp.int32)
    doubled = (device_ids + offset) % DEVICES
    dropped = (doubled + DEVICES // 2) % DEVICES
    counts = per_owner + (device_ids[None, :] == doubled[:, None]).astype(jnp.int32) - (device_ids[None, :] == dropped[:, None]).astype(jnp.int32)
    slot_all = jnp.arange(DEVICES * slots_each, dtype=jnp.int32)
    slot_owner = slot_all // slots_each
    slot_occur = slot_all % slots_each
    valid = slot_occur[None, :] < counts[:, slot_owner]
    scores = jax.random.randint(key_score, (DEVICES, DEVICES * slots_each), 0, 2 ** 19, dtype=jnp.int32) * (DEVICES * slots_each) + slot_all[None, :]
    scores = jnp.where(valid, scores, jnp.int32(2 ** 31 - 1))
    order = jnp.argsort(scores, axis=1, stable=True)[:, :requests_each].astype(jnp.int32)
    owners = order // slots_each
    occurs = order % slots_each
    shifts = jax.random.randint(key_local, (DEVICES,), 0, TB_DEV, dtype=jnp.int32)
    local_ids = (device_ids[:, None] * per_owner + occurs + shifts[owners]) % TB_DEV
    return (owners * TB_DEV + local_ids).reshape(DEVICES * SB_DEV, SUPP)


def place_ends(values, rng, smallest, top_value):
    longest = values.shape.index(max(values.shape))
    spots = []
    for shift in (0, 1):
        where = [jax.random.randint(jax.random.fold_in(rng, axis), (), 0, length) for axis, length in enumerate(values.shape)]
        where[longest] = (where[longest] + shift) % values.shape[longest]
        spots.append(tuple(where))
    return values.at[spots[0]].set(smallest).at[spots[1]].set(top_value)


def levels(stream_key, extent, shards, smallest, largest):
    factor_of, own = 1.0, jax.random.fold_in(stream_key, 6)
    for dim, blocks in shards:
        draws = jnp.exp(jax.random.uniform(jax.random.fold_in(own, dim), (blocks,), jnp.float32, smallest / len(shards), largest / len(shards)))
        factor_of = factor_of * jnp.repeat(draws, extent[dim] // blocks).reshape([-1 if axis == dim else 1 for axis in range(len(extent))])
    return factor_of


def setup_inputs(seed: int = 0) -> dict:
    key_of = jax.random.split(jax.random.key(seed), 10)
    src_cent = draw_src_cent(jax.random.fold_in(key_of[9], 71), 0)
    tgt_cent = draw_tgt_cent(jax.random.fold_in(key_of[9], 71), 0)
    src_mass = jnp.clip(jnp.exp(math.log(0.0009765625) - 2.7725887 * jax.random.uniform(key_of[2], (KS,), jnp.float32) ** levels(key_of[2], (KS,), ((0, 4),), -0.2, 0.2)), 6.103515625e-05, 0.0009765625)
    tgt_mass = jnp.clip(jnp.exp(math.log(0.0009765625) - 2.7725887 * jax.random.uniform(key_of[3], (KT,), jnp.float32) ** levels(key_of[3], (KT,), ((0, 32),), -0.2, 0.2)), 6.103515625e-05, 0.0009765625)
    src_pts = draw_src_pts(jax.random.fold_in(key_of[9], 71), 0)
    tgt_pts = draw_tgt_pts(jax.random.fold_in(key_of[9], 71), 0)
    src_cluster = place_ends(jax.random.randint(key_of[6], (NS,), 0, KS), jax.random.fold_in(key_of[6], 1), 0, KS - 1).astype(jnp.int32)
    tgt_cluster = place_ends(jax.random.randint(key_of[7], (NT,), 0, KT), jax.random.fold_in(key_of[7], 1), 0, KT - 1).astype(jnp.int32)
    support = draw_support(jax.random.fold_in(key_of[9], 71), 0)
    return {"src_cent": src_cent, "tgt_cent": tgt_cent, "src_mass": src_mass, "tgt_mass": tgt_mass, "src_pts": src_pts, "tgt_pts": tgt_pts, "src_cluster": src_cluster, "tgt_cluster": tgt_cluster, "support": support}


EPS = 0.1


def pair_cost(left_pts, right_pts):
    cross = jnp.einsum("fi,fj->ij", left_pts, right_pts, precision=lax.Precision.HIGHEST, preferred_element_type=jnp.float32)
    return jnp.sum(left_pts * left_pts, 0)[:, None] + jnp.sum(right_pts * right_pts, 0)[None, :] - 2.0 * cross


def reference(src_cent, tgt_cent, src_mass, tgt_mass, src_pts, tgt_pts, src_cluster, tgt_cluster, support):
    coarse_cost = pair_cost(src_cent, tgt_cent)
    log_src = jnp.log(src_mass)
    log_tgt = jnp.log(tgt_mass)
    coarse_g = jnp.zeros(coarse_cost.shape[1], jnp.float32)
    coarse_f = jnp.zeros(coarse_cost.shape[0], jnp.float32)
    for turn_index in range(ITERS):
        scores = log_tgt[None, :] + (coarse_g[None, :] - coarse_cost) / EPS
        maxima = jnp.max(scores, 1)
        coarse_f = -EPS * (maxima + jnp.log(jnp.sum(jnp.exp(scores - maxima[:, None]), 1)))
        scores = log_src[:, None] + (coarse_f[:, None] - coarse_cost) / EPS
        maxima = jnp.max(scores, 0)
        coarse_g = -EPS * (maxima + jnp.log(jnp.sum(jnp.exp(scores - maxima[None, :]), 0)))
    start_f = coarse_f[src_cluster]
    start_g = coarse_g[tgt_cluster]
    src_count = src_pts.shape[1] // BLK
    tgt_count = tgt_pts.shape[1] // BLK
    src_blocks = src_pts.reshape(F, src_count, BLK).transpose(1, 0, 2)
    tgt_blocks = tgt_pts.reshape(F, tgt_count, BLK).transpose(1, 0, 2)
    start_fb = start_f.reshape(src_count, BLK)
    start_gb = start_g.reshape(tgt_count, BLK)

    def one_block(carry, inputs):
        col_max, col_sum = carry
        src_block, src_dual, block_ids = inputs
        tgt_sel = tgt_blocks[block_ids]
        tgt_dual = start_gb[block_ids]
        cross = jnp.einsum("fi,kfj->ikj", src_block, tgt_sel, precision=lax.Precision.HIGHEST, preferred_element_type=jnp.float32)
        distance = jnp.sum(src_block * src_block, 0)[:, None, None] + jnp.sum(tgt_sel * tgt_sel, 1)[None, :, :] - 2.0 * cross
        scores = (tgt_dual[None, :, :] - distance) / EPS
        row_max = jnp.max(scores, (1, 2))
        row_term = -EPS * (row_max + jnp.log(jnp.sum(jnp.exp(scores - row_max[:, None, None]), (1, 2))) - jnp.log(float(SUPP * BLK)))
        scores = (src_dual[:, None, None] - distance) / EPS
        part_max = jnp.max(scores, 0)
        part_sum = jnp.sum(jnp.exp(scores - part_max[None]), 0)
        old_max = col_max[block_ids]
        new_max = jnp.maximum(old_max, part_max)
        new_sum = col_sum[block_ids] * jnp.exp(old_max - new_max) + part_sum * jnp.exp(part_max - new_max)
        col_max = col_max.at[block_ids].set(new_max)
        col_sum = col_sum.at[block_ids].set(new_sum)
        return (col_max, col_sum), row_term

    init = (jnp.full((tgt_count, BLK), -jnp.inf, jnp.float32), jnp.zeros((tgt_count, BLK), jnp.float32))
    (col_max, col_sum), row_terms = lax.scan(one_block, init, (src_blocks, start_fb, support))
    named = jnp.zeros(tgt_count, jnp.float32).at[support.reshape(-1)].add(jnp.ones(support.size, jnp.float32))
    col_term = -EPS * (col_max + jnp.log(col_sum) - jnp.log(named * BLK)[:, None])
    fine_f = 0.5 * (start_f + row_terms.reshape(-1))
    fine_g = 0.5 * (start_g + col_term.reshape(-1))
    return coarse_f, coarse_g, fine_f, fine_g
```

```python
import math

import jax
import jax.numpy as jnp
from jax import lax
from jax.experimental import pallas as pl
from jax.experimental.pallas import tpu as pltpu
from jax.sharding import PartitionSpec as P

MESH = pl.DeviceIdType.MESH
F = 16
BLK = 256
SUPP = 16
SB_DEV = 8
TB_DEV = 32
KS = 4096
KT = 4096
EPS = 0.1
KAPPA = math.log2(math.e) / EPS
UNIT = EPS * math.log(2.0)
DEV = 128
HALF = KS // 2
CH = 64
NJ = KT // 128
VMEM = pl.BlockSpec(memory_space=pltpu.VMEM)
SMEM = pl.BlockSpec(memory_space=pltpu.SMEM)
f32 = jnp.float32
i32 = jnp.int32
bf16 = jnp.bfloat16


def split3(v):
    hi = v.astype(bf16)
    rest = v - hi.astype(f32)
    mid = rest.astype(bf16)
    return hi, mid, (rest - mid.astype(f32)).astype(bf16)


def stack(pts, term, left):
    h, m, l = split3(pts)
    n = pts.shape[1]
    th, tm, tl = [v.astype(f32) for v in split3(term)]
    rid = lax.broadcasted_iota(i32, (16, n), 0)
    base, ones = (0, 3) if left else (3, 0)
    extra = jnp.where(rid == base, th, jnp.where(rid == base + 1, tm, jnp.where(rid == base + 2, tl, 0.0)))
    extra = jnp.where((rid >= ones) & (rid < ones + 3), 1.0, extra).astype(bf16)
    zero = jnp.zeros((16, n), bf16)
    if left:
        return jnp.concatenate([h, h, m, h, l, m, extra, zero], 0)
    return jnp.concatenate([h, m, h, l, h, m, extra, zero], 0)


def left_rows(x):
    term = -KAPPA * jnp.sum(x * x, 0, keepdims=True)
    return stack((2.0 * KAPPA) * x, term, True).astype(f32).T.astype(bf16)


def spread(row):
    return jnp.broadcast_to(row, (128, 128)).T


def block(j, width=128):
    return slice(j * width, (j + 1) * width)


def gather_kernel(src_ref, smass_ref, tgt_ref, tmass_ref, src_out, smass_out, tgt_out, tmass_out, ssem, rsem, lsem):
    row = lax.axis_index("row")
    col = lax.axis_index("col")
    core = lax.rem(col, 2)
    peers = [({"row": lax.rem(row + d, 4), "col": col}, d) for d in range(1, 4)]
    cpeers = [({"row": row, "col": lax.rem(col + d, 32)}, d) for d in range(1, 32)]
    barrier = pltpu.get_barrier_semaphore()
    for peer, _ in peers + cpeers:
        pl.semaphore_signal(barrier, inc=1, device_id=peer, device_id_type=MESH)
    pl.semaphore_wait(barrier, 34)
    half = pl.ds(pl.multiple_of(core * 512, 512), 512)
    copies = []
    for n, (peer, d) in enumerate(cpeers):
        for a, (src, dst) in enumerate(((tgt_ref, tgt_out), (tmass_ref, tmass_out))):
            copies.append(pltpu.make_async_remote_copy(
                src_ref=src, dst_ref=dst.at[col], send_sem=ssem.at[n, a], recv_sem=rsem.at[n, a],
                device_id=peer, device_id_type=MESH))
    for n, (peer, d) in enumerate(peers):
        for a, (src, dst) in enumerate(((src_ref, src_out), (smass_ref, smass_out))):
            copies.append(pltpu.make_async_remote_copy(
                src_ref=src.at[:, half], dst_ref=dst.at[row], send_sem=ssem.at[31 + n, a],
                recv_sem=rsem.at[31 + n, a], device_id=peer, device_id_type=MESH))
    for c in copies:
        c.start()
    local = [pltpu.make_async_copy(tgt_ref, tgt_out.at[col], lsem.at[0]),
             pltpu.make_async_copy(tmass_ref, tmass_out.at[col], lsem.at[1]),
             pltpu.make_async_copy(src_ref.at[:, half], src_out.at[row], lsem.at[2]),
             pltpu.make_async_copy(smass_ref.at[:, half], smass_out.at[row], lsem.at[3])]
    for c in local:
        c.start()
    for c in local + copies:
        c.wait()


def gather_centroids(src_cent, src_mass, tgt_cent, tgt_mass):
    return pl.pallas_call(
        gather_kernel,
        out_shape=(jax.ShapeDtypeStruct((4, F, 512), f32), jax.ShapeDtypeStruct((4, 1, 512), f32),
                   jax.ShapeDtypeStruct((32, F, 128), f32), jax.ShapeDtypeStruct((32, 1, 128), f32)),
        in_specs=[VMEM] * 4,
        out_specs=(VMEM,) * 4,
        scratch_shapes=[pltpu.SemaphoreType.DMA((34, 2)), pltpu.SemaphoreType.DMA((34, 2)),
                        pltpu.SemaphoreType.DMA((4,))],
        compiler_params=pltpu.CompilerParams(collective_id=0, has_side_effects=True),
        name="gather_centroids",
    )(src_cent, src_mass.reshape(1, -1), tgt_cent, tgt_mass.reshape(1, -1))


def sinkhorn_kernel(src_ref, smass_ref, tgt_ref, tmass_ref, ftab_ref, gtab_ref,
                    a_scr, d0, d1, t0, t1, ys, xs, gp, lb, acc, fst, am, sbuf, rbuf, fs_buf, fr_buf,
                    send_sem, recv_sem, fsend, frecv):
    row = lax.axis_index("row")
    col = lax.axis_index("col")
    core = lax.rem(col, 2)
    partner = {"row": row, "col": col + 1 - 2 * core}
    barrier = pltpu.get_barrier_semaphore()
    pl.semaphore_signal(barrier, inc=1, device_id=partner, device_id_type=MESH)
    pl.semaphore_wait(barrier, 1)
    for k in range(32):
        y = tgt_ref[k]
        lbk = jnp.log2(tmass_ref[k])
        ys[:, block(k)] = stack(y, lbk - KAPPA * jnp.sum(y * y, 0, keepdims=True), False)
        lb[:, block(k)] = jnp.broadcast_to(lbk, (8, 128))
    for q in range(4):
        for h in range(4):
            r0 = q * 512 + h * 128
            xs[r0:r0 + 128, :] = left_rows(src_ref[q, :, block(h)])
            am[r0:r0 + 128, :] = spread(smass_ref[q, :, block(h)])
    acc[...] = jnp.full_like(acc, -jnp.inf)

    def product(dst, b, quarter):
        xc = xs[pl.ds(pl.multiple_of(b * 256, 256), 256), :]
        for u in range(2):
            c0 = quarter * 1024 + u * 512
            dst[:, c0:c0 + 512] = jnp.dot(xc, ys[:, c0:c0 + 512], preferred_element_type=f32)

    def first(src, b, quarter):
        rr = block(quarter, CH)
        mx = src[rr, block(0)]
        for j in range(1, NJ):
            mx = jnp.maximum(mx, src[rr, block(j)])
        mx = jnp.broadcast_to(jnp.max(mx, 1, keepdims=True), (CH, 128))
        s = jnp.exp2(src[rr, block(0)] - mx)
        for j in range(1, NJ):
            s = s + jnp.exp2(src[rr, block(j)] - mx)
        s = jnp.broadcast_to(jnp.sum(s, 1, keepdims=True), (CH, 128))
        f1 = -(mx + jnp.log2(s))
        rows = pl.ds(pl.multiple_of(b * 256 + quarter * CH, CH), CH)
        fst[rows, :] = f1
        fl = f1 + jnp.log2(am[rows, :])
        for j in range(NJ):
            v = src[rr, block(j)] + fl
            a_scr[rows, block(j)] = v
            acc[:, block(j)] = jnp.maximum(acc[:, block(j)], jnp.max(v.reshape(CH // 8, 8, 128), 0))

    for quarter in range(4):
        product(d0, 0, quarter)

    def pair(p, _):
        for quarter in range(4):
            product(d1, 2 * p + 1, quarter)
            first(d0, 2 * p, quarter)
        for quarter in range(4):
            product(d0, lax.rem(2 * p + 2, 8), quarter)
            first(d1, 2 * p + 1, quarter)
        return 0

    lax.fori_loop(0, 4, pair, 0)
    for j in range(NJ):
        gp[:, block(j)] = jnp.broadcast_to(jnp.max(acc[:, block(j)], 0, keepdims=True), (8, 128))
    acc[...] = jnp.zeros_like(acc)

    def second(c, _):
        rows = pl.ds(pl.multiple_of(c * CH, CH), CH)
        for j in range(NJ):
            v = a_scr[rows, block(j)].reshape(CH // 8, 8, 128) - gp[:, block(j)][None]
            acc[:, block(j)] = acc[:, block(j)] + jnp.sum(jnp.exp2(v), 0)
        return 0

    lax.fori_loop(0, HALF // CH, second, 0)
    for j in range(NJ):
        sbuf[0, :, block(j)] = gp[:1, block(j)] + jnp.log2(jnp.sum(acc[:, block(j)], 0, keepdims=True))

    def swap(k):
        cp = pltpu.make_async_remote_copy(src_ref=sbuf.at[k], dst_ref=rbuf.at[k], send_sem=send_sem.at[k],
                                          recv_sem=recv_sem.at[k], device_id=partner, device_id_type=MESH)
        cp.start()
        cp.wait()

    swap(0)
    for j in range(NJ):
        l0, l1 = sbuf[0, :, block(j)], rbuf[0, :, block(j)]
        m = jnp.maximum(l0, l1)
        l = m + jnp.log2(jnp.exp2(l0 - m) + jnp.exp2(l1 - m))
        gp[:, block(j)] = lb[:, block(j)] - jnp.broadcast_to(l, (8, 128))

    def turn(k, restab, last):
        acc[...] = jnp.zeros_like(acc)

        def scores(t, rows):
            r = None
            for j in range(NJ):
                v = a_scr[rows, block(j)].reshape(CH // 8, 8, 128) + gp[:, block(j)][None]
                e = jnp.exp2(v).reshape(CH, 128)
                t[:, block(j)] = e
                r = e if r is None else r + e
            return jnp.broadcast_to(jnp.sum(r, 1, keepdims=True), (CH, 128))

        def sums(t, rows, r):
            u = am[rows, :] / r
            if restab or last:
                step = -jnp.log2(u)
                fst[rows, :] = fst[rows, :] - step
            for j in range(NJ):
                acc[:, block(j)] = acc[:, block(j)] + jnp.sum((t[:, block(j)] * u).reshape(CH // 8, 8, 128), 0)
                if restab:
                    a_scr[rows, block(j)] = a_scr[rows, block(j)] - step

        def chunk(c, _):
            ra = pl.ds(pl.multiple_of(c * 2 * CH, CH), CH)
            rb = pl.ds(pl.multiple_of(c * 2 * CH + CH, CH), CH)
            sa = scores(t0, ra)
            sb = scores(t1, rb)
            sums(t0, ra, sa)
            sums(t1, rb, sb)
            return 0

        lax.fori_loop(0, HALF // CH // 2, chunk, 0)
        for j in range(NJ):
            sbuf[k, :, block(j)] = jnp.sum(acc[:, block(j)], 0, keepdims=True)
        swap(k)
        for j in range(NJ):
            c = jnp.broadcast_to(sbuf[k, :, block(j)] + rbuf[k, :, block(j)], (8, 128))
            gp[:, block(j)] = gp[:, block(j)] + (lb[:, block(j)] - jnp.log2(c))

    def two(p, _):
        turn(2 * p + 1, False, False)
        turn(2 * p + 2, True, False)
        return 0

    lax.fori_loop(0, 3, two, 0)
    turn(7, False, True)
    for h in range(16):
        fs_buf[h:h + 1, :] = (fst[block(h), :] * UNIT).T[:1, :]
    cp = pltpu.make_async_remote_copy(src_ref=fs_buf, dst_ref=fr_buf, send_sem=fsend, recv_sem=frecv,
                                      device_id=partner, device_id_type=MESH)
    cp.start()
    for j in range(NJ):
        gtab_ref[j:j + 1, :] = gp[:1, block(j)] * UNIT
    cp.wait()
    for q in range(4):
        a, b = fs_buf[q * 4:q * 4 + 4], fr_buf[q * 4:q * 4 + 4]
        ftab_ref[q * 8:q * 8 + 4, :] = jnp.where(core == 0, a, b)
        ftab_ref[q * 8 + 4:q * 8 + 8, :] = jnp.where(core == 0, b, a)


def sinkhorn(src_all, smass_all, tgt_all, tmass_all):
    V = pltpu.VMEM
    dma = pltpu.SemaphoreType.DMA
    return pl.pallas_call(
        sinkhorn_kernel,
        out_shape=(jax.ShapeDtypeStruct((32, 128), f32), jax.ShapeDtypeStruct((32, 128), f32)),
        in_specs=[VMEM] * 4,
        out_specs=(VMEM, VMEM),
        scratch_shapes=[V((HALF, KT), f32), V((256, KT), f32), V((256, KT), f32), V((CH, KT), f32), V((CH, KT), f32),
                        V((128, KT), bf16), V((HALF, 128), bf16), V((8, KT), f32), V((8, KT), f32), V((8, KT), f32),
                        V((HALF, 128), f32), V((HALF, 128), f32), V((8, 1, KT), f32), V((8, 1, KT), f32),
                        V((16, 128), f32), V((16, 128), f32), dma((8,)), dma((8,)), dma, dma],
        compiler_params=pltpu.CompilerParams(collective_id=1, has_side_effects=True,
                                             vmem_limit_bytes=60 * 1024 * 1024),
        cost_estimate=pl.CostEstimate(flops=60_000_000_000, bytes_accessed=1 << 20, transcendentals=1 << 26),
        name="sinkhorn",
    )(src_all, smass_all, tgt_all, tmass_all)


def request_kernel(sup_ref, req_ref, slot_ref):
    wanted = sup_ref[...].astype(f32)
    owner = jnp.floor(wanted * (1.0 / TB_DEV))
    local = wanted - owner * TB_DEV
    sub = lax.broadcasted_iota(i32, (128, 128), 0)
    lane = lax.broadcasted_iota(i32, (128, 128), 1)
    lanef = lane.astype(f32)
    same = jnp.broadcast_to(owner, (128, 128)) == sub.astype(f32)
    lo = jnp.min(jnp.where(same, lanef, 1e6), 1, keepdims=True)
    hi = jnp.max(jnp.where(same, lanef, -1.0), 1, keepdims=True)
    locb = jnp.broadcast_to(local, (128, 128)) + 1.0
    id0 = jnp.sum(jnp.where(lanef == lo, locb, 0.0), 1, keepdims=True) - 1.0
    id1 = jnp.sum(jnp.where((lanef == hi) & (hi > lo), locb, 0.0), 1, keepdims=True) - 1.0
    req_ref[...] = jnp.where(lane == 0, id0, jnp.where(lane == 1, id1, 0.0)).astype(i32)
    ownc = spread(owner)
    before = jnp.where((ownc == jnp.broadcast_to(owner, (128, 128))) & (sub < lane), 1.0, 0.0)
    slot_ref[...] = (owner * 2.0 + jnp.sum(before, 0, keepdims=True)).astype(i32)


def make_requests(support):
    return pl.pallas_call(
        request_kernel,
        out_shape=(jax.ShapeDtypeStruct((128, 128), i32), jax.ShapeDtypeStruct((1, 128), i32)),
        in_specs=[VMEM], out_specs=(VMEM, VMEM), name="make_requests",
    )(support.reshape(1, 128))


def pick_kernel(inc_ref, pts_ref, clu_ref, pts_out, clu_out):
    def one(p, _):
        for q in range(2):
            t = jnp.maximum(inc_ref[p, q], 0)
            pts_out[p, q] = pts_ref[:, pl.ds(pl.multiple_of(t * BLK, BLK), BLK)]
            clu_out[p, 2 * q:2 * q + 2, :] = clu_ref[t]
        return 0

    lax.fori_loop(0, DEV, one, 0)


def pick(incoming, tgt_pts, tgt_cluster):
    return pl.pallas_call(
        pick_kernel,
        out_shape=(jax.ShapeDtypeStruct((DEV, 2, F, BLK), f32), jax.ShapeDtypeStruct((DEV, 4, 128), i32)),
        in_specs=[SMEM, VMEM, VMEM], out_specs=(VMEM, VMEM), name="pick",
    )(incoming, tgt_pts, tgt_cluster.reshape(TB_DEV, 2, 128))


def lookup(tab, idx):
    low = idx & 127
    high = idx >> 7
    out = jnp.zeros((8, 128), f32)
    for r in range(32):
        got = jnp.take_along_axis(jnp.broadcast_to(tab[r:r + 1, :], (8, 128)), low, axis=1)
        out = jnp.where(high == r, got, out)
    return out


def fine_kernel(slot_ref, ftab_ref, gtab_ref, src_ref, sclu_ref, tgt_ref, tclu_ref, oclu_ref,
                cf_ref, cg_ref, ff_ref, sg_ref, back_ref, gs, fs, xt, fx, sc, rm):
    row = lax.axis_index("row")
    col = lax.axis_index("col")
    cf_ref[...] = ftab_ref[pl.ds(pl.multiple_of(row * 8, 8), 8), :]
    cg_ref[...] = gtab_ref[pl.ds(col, 1), :]
    ft = ftab_ref[...] * KAPPA
    gt = gtab_ref[...] * KAPPA
    for r in range(2):
        fs[block(r, 8), :] = lookup(ft, sclu_ref[block(r, 8), :])

    def own(r, _):
        rows = pl.ds(pl.multiple_of(r * 8, 8), 8)
        sg_ref[rows, :] = lookup(gt, oclu_ref[rows, :]) * UNIT
        return 0

    lax.fori_loop(0, 8, own, 0)

    def sent(r, _):
        rows = pl.ds(pl.multiple_of(r * 8, 8), 8)
        gs[rows, :] = lookup(gt, tclu_ref[rows, :])
        return 0

    lax.fori_loop(0, 64, sent, 0)

    def one_block(b, _):
        for h in range(2):
            cols = pl.ds(pl.multiple_of(b * BLK + h * 128, 128), 128)
            xt[block(h), :] = left_rows(src_ref[:, cols])
            fx[block(h), :] = spread(fs[pl.ds(2 * b + h, 1), :])
        rm[...] = jnp.full_like(rm, -jnp.inf)

        def some(g, _):
            for u in range(2):
                k = 2 * g + u
                slot = slot_ref[b * SUPP + k]
                y = tgt_ref[slot]
                gj = jnp.concatenate([gs[pl.ds(2 * slot, 1), :], gs[pl.ds(2 * slot + 1, 1), :]], 1)
                st = stack(y, gj - KAPPA * jnp.sum(y * y, 0, keepdims=True), False)
                d = jnp.dot(xt[...], st, preferred_element_type=f32)
                sc[k] = d
                rm[...] = jnp.maximum(rm[...], jnp.maximum(d[:, :128], d[:, 128:]))
                for h in range(2):
                    v = d[:, block(h)] + fx[...]
                    m = jnp.max(v, 0, keepdims=True)
                    s = jnp.sum(jnp.exp2(v - m), 0, keepdims=True)
                    back_ref[pl.ds(2 * slot + h, 1), :] = m + jnp.log2(s) - gj[:, block(h)]
            return 0

        lax.fori_loop(0, SUPP // 2, some, 0)
        m = jnp.broadcast_to(jnp.max(rm[...], 1, keepdims=True), (BLK, 128))
        rm[...] = m

        def total(k, s):
            d = sc[k]
            return s + jnp.exp2(d[:, :128] - rm[...]) + jnp.exp2(d[:, 128:] - rm[...])

        s = lax.fori_loop(0, SUPP, total, jnp.zeros((BLK, 128), f32))
        lse = rm[...] + jnp.log2(jnp.sum(s, 1, keepdims=True)) - math.log2(SUPP * BLK)
        out = (0.5 * UNIT) * (fx[...] - lse)
        for h in range(2):
            ff_ref[pl.ds(2 * b + h, 1), :] = out[block(h), :].T[:1, :]
        return 0

    lax.fori_loop(0, SB_DEV, one_block, 0)


def fine(slots, ftab, gtab, src_pts, src_cluster, tiles, tclu, tgt_cluster):
    S = jax.ShapeDtypeStruct
    V = pltpu.VMEM
    return pl.pallas_call(
        fine_kernel,
        out_shape=(S((8, 128), f32), S((1, 128), f32), S((16, 128), f32), S((64, 128), f32), S((4 * DEV, 128), f32)),
        in_specs=[SMEM] + [VMEM] * 7,
        out_specs=(VMEM,) * 5,
        scratch_shapes=[V((4 * DEV, 128), f32), V((16, 128), f32), V((BLK, 128), bf16), V((BLK, 128), f32),
                        V((SUPP, BLK, BLK), f32), V((BLK, 128), f32)],
        name="fine",
    )(slots, ftab, gtab, src_pts, src_cluster.reshape(16, 128), tiles, tclu, tgt_cluster.reshape(64, 128))


def column_kernel(inc_ref, ret_ref, sg_ref, fg_ref, idr):
    for q in range(2):
        idr[q] = jnp.broadcast_to(inc_ref[:, q:q + 1].astype(f32), (DEV, 128))

    def one(t, _):
        tf = t.astype(f32)
        masks = [idr[q] == tf for q in range(2)]
        count = sum(jnp.sum(jnp.where(m, 1.0, 0.0), 0, keepdims=True) for m in masks)
        for h in range(2):
            vs = [ret_ref[pl.ds(2 * q + h, DEV, stride=4), :] for q in range(2)]
            m = [jnp.max(jnp.where(masks[q], vs[q], -jnp.inf), 0, keepdims=True) for q in range(2)]
            m = jnp.maximum(m[0], m[1])
            s = sum(jnp.sum(jnp.where(masks[q], jnp.exp2(vs[q] - m), 0.0), 0, keepdims=True) for q in range(2))
            lse = m + jnp.log2(s) - jnp.log2(count * BLK)
            fg_ref[pl.ds(2 * t + h, 1), :] = 0.5 * (sg_ref[pl.ds(2 * t + h, 1), :] - UNIT * lse)
        return 0

    lax.fori_loop(0, TB_DEV, one, 0)


def columns(incoming, ret, start_g):
    return pl.pallas_call(
        column_kernel,
        out_shape=jax.ShapeDtypeStruct((64, 128), f32),
        in_specs=[VMEM] * 3, out_specs=VMEM,
        scratch_shapes=[pltpu.VMEM((2, DEV, 128), f32)],
        name="columns",
    )(incoming, ret, start_g)


def exchange(x):
    return lax.all_to_all(x, ("row", "col"), split_axis=0, concat_axis=0, tiled=True)


def on_device(src_cent, tgt_cent, src_mass, tgt_mass, src_pts, tgt_pts, src_cluster, tgt_cluster, support):
    req, slots = make_requests(support)
    incoming = exchange(req)
    send_pts, send_clu = pick(incoming, tgt_pts, tgt_cluster)
    tiles = exchange(send_pts)
    tclu = exchange(send_clu)
    ftab, gtab = sinkhorn(*gather_centroids(src_cent, src_mass, tgt_cent, tgt_mass))
    cf, cg, ff, sg, back = fine(slots.reshape(128), ftab, gtab, src_pts, src_cluster,
                                tiles.reshape(2 * DEV, F, BLK), tclu.reshape(4 * DEV, 128), tgt_cluster)
    ret = exchange(back.reshape(DEV, 4, 128)).reshape(4 * DEV, 128)
    fg = columns(incoming, ret, sg)
    return cf.reshape(-1), cg.reshape(-1), ff.reshape(-1), fg.reshape(-1)


def solution(mesh):
    both = ("row", "col")
    in_specs = (P(None, "row"), P(None, "col"), P("row"), P("col"), P(None, both), P(None, both), P(both), P(both),
                P(both, None))
    out_specs = (P("row"), P("col"), P(both), P(both))
    return jax.shard_map(on_device, mesh=mesh, in_specs=in_specs, out_specs=out_specs, check_vma=False)
```

```python
import math

import jax
import jax.numpy as jnp
from jax import lax
from jax.experimental import pallas as pl
from jax.experimental.pallas import tpu as pltpu
from jax.sharding import PartitionSpec as P

MESH = pl.DeviceIdType.MESH
F = 16
BLK = 256
SUPP = 16
SB_DEV = 8
TB_DEV = 32
KS = 4096
KT = 4096
EPS = 0.1
KAPPA = math.log2(math.e) / EPS
UNIT = EPS * math.log(2.0)
DEV = 128
HALF = KS // 2
CH = 64
NJ = KT // 128
VMEM = pl.BlockSpec(memory_space=pltpu.VMEM)
SMEM = pl.BlockSpec(memory_space=pltpu.SMEM)
f32 = jnp.float32
i32 = jnp.int32
bf16 = jnp.bfloat16


def split3(v):
    hi = v.astype(bf16)
    rest = v - hi.astype(f32)
    mid = rest.astype(bf16)
    return hi, mid, (rest - mid.astype(f32)).astype(bf16)


def stack(pts, term, left):
    h, m, l = split3(pts)
    n = pts.shape[1]
    th, tm, tl = [v.astype(f32) for v in split3(term)]
    rid = lax.broadcasted_iota(i32, (16, n), 0)
    base, ones = (0, 3) if left else (3, 0)
    extra = jnp.where(rid == base, th, jnp.where(rid == base + 1, tm, jnp.where(rid == base + 2, tl, 0.0)))
    extra = jnp.where((rid >= ones) & (rid < ones + 3), 1.0, extra).astype(bf16)
    zero = jnp.zeros((16, n), bf16)
    if left:
        return jnp.concatenate([h, h, m, h, l, m, extra, zero], 0)
    return jnp.concatenate([h, m, h, l, h, m, extra, zero], 0)


def left_rows(x):
    term = -KAPPA * jnp.sum(x * x, 0, keepdims=True)
    return stack((2.0 * KAPPA) * x, term, True).astype(f32).T.astype(bf16)


def spread(row):
    return jnp.broadcast_to(row, (128, 128)).T


def block(j, width=128):
    return slice(j * width, (j + 1) * width)


def place(index):
    return {"row": index // 32, "col": lax.rem(index, 32)}


def remote(src, dst, ssem, rsem, where):
    return pltpu.make_async_remote_copy(src_ref=src, dst_ref=dst, send_sem=ssem, recv_sem=rsem, device_id=where,
                                        device_id_type=MESH)


def each(n, body):
    def step(i, c):
        body(i)
        return c

    lax.fori_loop(0, n, step, 0)


def coarse_kernel(src_in, smass_in, tgt_in, tmass_in, req_ref, pts_ref, clu_ref,
                  ftab_ref, gtab_ref, tiles_ref, inc_ref,
                  src_all, smass_all, tgt_all, tmass_all, inc_s, blocks, out_buf,
                  a_scr, d0, d1, t0, t1, ys, xs, gp, lb, acc, fst, am, mxs, fls, rs, sbuf, rbuf, fs_buf, fr_buf,
                  send_sem, recv_sem, fsend, frecv, cs_sem, cr_sem, qs_sem, qr_sem, bs_sem, br_sem, lsem):
    row = lax.axis_index("row")
    col = lax.axis_index("col")
    me = row * 32 + col
    core = lax.rem(col, 2)
    partner = {"row": row, "col": col + 1 - 2 * core}
    barrier = pltpu.get_barrier_semaphore()
    each(DEV - 1, lambda d: pl.semaphore_signal(barrier, inc=1, device_id=place(lax.rem(me + d + 1, DEV)),
                                                device_id_type=MESH))
    half = pl.ds(pl.multiple_of(core * 512, 512), 512)

    def tgt_copy(d, a):
        where = {"row": row, "col": lax.rem(col + d + 1, 32)}
        src, dst = ((tgt_in, tgt_all), (tmass_in, tmass_all))[a]
        return remote(src, dst.at[col], cs_sem.at[d, a], cr_sem.at[d, a], where)

    def src_copy(d, a):
        where = {"row": lax.rem(row + d + 1, 4), "col": col}
        src, dst = ((src_in, src_all), (smass_in, smass_all))[a]
        return remote(src.at[:, half], dst.at[row], cs_sem.at[31 + d, a], cr_sem.at[31 + d, a], where)

    def req_copy(d):
        to = lax.rem(me + d + 1, DEV)
        return remote(req_ref.at[to], inc_ref.at[me], qs_sem.at[d], qr_sem.at[d], place(to))

    def blk_copy(d):
        to = lax.rem(me + d + 1, DEV)
        return remote(out_buf.at[to], tiles_ref.at[me], bs_sem.at[d], br_sem.at[d], place(to))

    local = [pltpu.make_async_copy(tgt_in, tgt_all.at[col], lsem.at[0]),
             pltpu.make_async_copy(tmass_in, tmass_all.at[col], lsem.at[1]),
             pltpu.make_async_copy(src_in.at[:, half], src_all.at[row], lsem.at[2]),
             pltpu.make_async_copy(smass_in.at[:, half], smass_all.at[row], lsem.at[3]),
             pltpu.make_async_copy(req_ref.at[me], inc_ref.at[me], lsem.at[4])]
    for c in local:
        c.start()
    pl.semaphore_wait(barrier, DEV - 1)

    def start_src(d):
        src_copy(d, 0).start()
        src_copy(d, 1).start()

    def start_tgt(d):
        tgt_copy(d, 0).start()
        tgt_copy(d, 1).start()

    def wait_src(d):
        src_copy(d, 0).wait()
        src_copy(d, 1).wait()

    def wait_tgt(d):
        tgt_copy(d, 0).wait()
        tgt_copy(d, 1).wait()

    each(3, start_src)
    each(31, start_tgt)
    each(DEV - 1, lambda d: req_copy(d).start())
    for c in local:
        c.wait()
    each(3, wait_src)
    each(31, wait_tgt)
    for k in range(32):
        y = tgt_all[k]
        lbk = jnp.log2(tmass_all[k])
        ys[:, block(k)] = stack(y, lbk - KAPPA * jnp.sum(y * y, 0, keepdims=True), False)
        lb[:, block(k)] = jnp.broadcast_to(lbk, (8, 128))
    for q in range(4):
        for h in range(4):
            r0 = q * 512 + h * 128
            xs[r0:r0 + 128, :] = left_rows(src_all[q, :, block(h)])
            am[r0:r0 + 128, :] = spread(smass_all[q, :, block(h)])

    for t in range(TB_DEV):
        for h in range(2):
            blocks[t, h * 16:h * 16 + 16, :] = pts_ref[:, block(2 * t + h)]
    each(DEV - 1, lambda d: req_copy(d).wait())
    to_scalar = pltpu.make_async_copy(inc_ref, inc_s, lsem.at[5])
    to_scalar.start()
    to_scalar.wait()

    def fill(p):
        for q in range(2):
            t = inc_s[p, 0, 4 + q]
            out_buf[p, q * 32:q * 32 + 32, :] = blocks[t]
            out_buf[p, 64 + 2 * q:66 + 2 * q, :] = clu_ref[t].astype(f32)
        out_buf[p, 68:72, :] = jnp.zeros((4, 128), f32)

    each(DEV, fill)
    each(DEV - 1, lambda d: blk_copy(d).start())
    own = pltpu.make_async_copy(out_buf.at[me], tiles_ref.at[me], lsem.at[6])
    own.start()

    acc[...] = jnp.full_like(acc, -jnp.inf)
    d1[192:, :] = jnp.zeros((CH, KT), f32)
    fls[...] = jnp.full_like(fls, -jnp.inf)

    def product(dst, b, quarter):
        xc = xs[pl.ds(pl.multiple_of(b * 256, 256), 256), :]
        for u in range(4):
            c0 = quarter * 1024 + u * 256
            dst[:, c0:c0 + 256] = jnp.dot(xc, ys[:, c0:c0 + 256], preferred_element_type=f32)

    def rows_of(n):
        return pl.ds(pl.multiple_of(n * CH, CH), CH)

    def top(src, q):
        rr = block(q, CH)
        mx = src[rr, block(0)]
        for j in range(1, NJ):
            mx = jnp.maximum(mx, src[rr, block(j)])
        mxs[...] = jnp.broadcast_to(jnp.max(mx, 1, keepdims=True), (CH, 128))

    def keep(src, q, rows, fl, j):
        v = src[block(q, CH), block(j)] + fl
        a_scr[rows, block(j)] = v
        acc[:, block(j)] = jnp.maximum(acc[:, block(j)], jnp.max(v.reshape(CH // 8, 8, 128), 0))

    def step(n, q, now, before, b_next, nxt, after, q_after):
        prev = rows_of(lax.rem(n + 31, 32))
        mx = mxs[...]
        fl = fls[...]
        s = None
        for j in range(NJ):
            e = jnp.exp2(now[block(q, CH), block(j)] - mx)
            s = e if s is None else s + e
            keep(before, (q + 3) % 4, prev, fl, j)
        product(nxt, b_next, q)
        s = jnp.broadcast_to(jnp.sum(s, 1, keepdims=True), (CH, 128))
        f1 = -(mx + jnp.log2(s))
        fst[rows_of(n), :] = f1
        fls[...] = f1 + jnp.log2(am[rows_of(n), :])
        top(after, q_after)

    for q in range(4):
        product(d0, 0, q)
    top(d0, 0)

    def pair(p):
        for q in range(4):
            step(8 * p + q, q, d0, d1 if q == 0 else d0, 2 * p + 1, d1, d1 if q == 3 else d0, (q + 1) % 4)
        for q in range(4):
            step(8 * p + 4 + q, q, d1, d0 if q == 0 else d1, lax.rem(2 * p + 2, 8), d0, d0 if q == 3 else d1,
                 (q + 1) % 4)

    each(4, pair)
    fl = fls[...]
    for j in range(NJ):
        keep(d1, 3, rows_of(31), fl, j)
    for j in range(NJ):
        gp[:, block(j)] = jnp.broadcast_to(jnp.max(acc[:, block(j)], 0, keepdims=True), (8, 128))
    acc[...] = jnp.zeros_like(acc)

    def second(c):
        for j in range(NJ):
            v = a_scr[rows_of(c), block(j)].reshape(CH // 8, 8, 128) - gp[:, block(j)][None]
            acc[:, block(j)] = acc[:, block(j)] + jnp.sum(jnp.exp2(v), 0)

    each(HALF // CH, second)
    for j in range(NJ):
        sbuf[0, :, block(j)] = gp[:1, block(j)] + jnp.log2(jnp.sum(acc[:, block(j)], 0, keepdims=True))

    def swap(k):
        cp = remote(sbuf.at[k], rbuf.at[k], send_sem.at[k], recv_sem.at[k], partner)
        cp.start()
        cp.wait()

    swap(0)
    for j in range(NJ):
        l0, l1 = sbuf[0, :, block(j)], rbuf[0, :, block(j)]
        m = jnp.maximum(l0, l1)
        l = m + jnp.log2(jnp.exp2(l0 - m) + jnp.exp2(l1 - m))
        gp[:, block(j)] = lb[:, block(j)] - jnp.broadcast_to(l, (8, 128))

    def turn(k, restab, last):
        acc[...] = jnp.zeros_like(acc)

        def score(t, rows, j):
            v = a_scr[rows, block(j)].reshape(CH // 8, 8, 128) + gp[:, block(j)][None]
            e = jnp.exp2(v).reshape(CH, 128)
            t[:, block(j)] = e
            return e

        def both(tn, rn, tp, rp):
            r = rs[...]
            u = am[rp, :] / jnp.broadcast_to(jnp.sum(r, 1, keepdims=True), (CH, 128))
            if restab or last:
                shift = -jnp.log2(u)
                fst[rp, :] = fst[rp, :] - shift
            r = None
            for j in range(NJ):
                e = score(tn, rn, j)
                r = e if r is None else r + e
                acc[:, block(j)] = acc[:, block(j)] + jnp.sum((tp[:, block(j)] * u).reshape(CH // 8, 8, 128), 0)
                if restab:
                    a_scr[rp, block(j)] = a_scr[rp, block(j)] - shift
            rs[...] = r

        r = score(t0, rows_of(0), 0)
        for j in range(1, NJ):
            r = r + score(t0, rows_of(0), j)
        rs[...] = r

        def chunk(c):
            both(t1, rows_of(2 * c + 1), t0, rows_of(2 * c))
            both(t0, rows_of(lax.rem(2 * c + 2, 32)), t1, rows_of(2 * c + 1))

        each(HALF // CH // 2, chunk)
        for j in range(NJ):
            sbuf[k, :, block(j)] = jnp.sum(acc[:, block(j)], 0, keepdims=True)
        swap(k)
        for j in range(NJ):
            c = jnp.broadcast_to(sbuf[k, :, block(j)] + rbuf[k, :, block(j)], (8, 128))
            gp[:, block(j)] = gp[:, block(j)] + (lb[:, block(j)] - jnp.log2(c))

    each(2, lambda i: turn(i + 1, False, False))
    turn(3, True, False)
    each(3, lambda i: turn(i + 4, False, False))
    turn(7, False, True)
    for h in range(16):
        fs_buf[h:h + 1, :] = (fst[block(h), :] * UNIT).T[:1, :]
    cp = remote(fs_buf, fr_buf, fsend, frecv, partner)
    cp.start()
    for j in range(NJ):
        gtab_ref[j:j + 1, :] = gp[:1, block(j)] * UNIT
    cp.wait()
    for q in range(4):
        a, b = fs_buf[q * 4:q * 4 + 4], fr_buf[q * 4:q * 4 + 4]
        ftab_ref[q * 8:q * 8 + 4, :] = jnp.where(core == 0, a, b)
        ftab_ref[q * 8 + 4:q * 8 + 8, :] = jnp.where(core == 0, b, a)
    own.wait()
    each(DEV - 1, lambda d: blk_copy(d).wait())


def coarse(src_cent, src_mass, tgt_cent, tgt_mass, req, tgt_pts, tgt_cluster):
    V = pltpu.VMEM
    S = jax.ShapeDtypeStruct
    dma = pltpu.SemaphoreType.DMA
    return pl.pallas_call(
        coarse_kernel,
        out_shape=(S((32, 128), f32), S((32, 128), f32), S((DEV, 72, 128), f32), S((DEV, 1, 128), i32)),
        in_specs=[VMEM] * 7,
        out_specs=(VMEM, VMEM, pl.BlockSpec(memory_space=pl.ANY), VMEM),
        scratch_shapes=[V((4, F, 512), f32), V((4, 1, 512), f32), V((32, F, 128), f32), V((32, 1, 128), f32),
                        pltpu.SMEM((DEV, 1, 128), i32), V((TB_DEV, 32, 128), f32), V((DEV, 72, 128), f32),
                        V((HALF, KT), f32), V((256, KT), f32), V((256, KT), f32), V((CH, KT), f32), V((CH, KT), f32),
                        V((128, KT), bf16), V((HALF, 128), bf16), V((8, KT), f32), V((8, KT), f32), V((8, KT), f32),
                        V((HALF, 128), f32), V((HALF, 128), f32), V((CH, 128), f32), V((CH, 128), f32),
                        V((CH, 128), f32), V((8, 1, KT), f32), V((8, 1, KT), f32),
                        V((16, 128), f32), V((16, 128), f32), dma((8,)), dma((8,)), dma, dma,
                        dma((34, 2)), dma((34, 2)), dma((DEV,)), dma((DEV,)), dma((DEV,)), dma((DEV,)), dma((7,))],
        compiler_params=pltpu.CompilerParams(collective_id=1, has_side_effects=True,
                                             vmem_limit_bytes=62 * 1024 * 1024),
        name="coarse",
    )(src_cent, src_mass.reshape(1, -1), tgt_cent, tgt_mass.reshape(1, -1), req, tgt_pts,
      tgt_cluster.reshape(TB_DEV, 2, 128))


def request_kernel(sup_ref, req_ref, slot_ref):
    wanted = sup_ref[...].astype(f32)
    owner = jnp.floor(wanted * (1.0 / TB_DEV))
    local = wanted - owner * TB_DEV
    sub = lax.broadcasted_iota(i32, (128, 128), 0)
    lane = lax.broadcasted_iota(i32, (128, 128), 1)
    lanef = lane.astype(f32)
    same = jnp.broadcast_to(owner, (128, 128)) == sub.astype(f32)
    lo = jnp.min(jnp.where(same, lanef, 1e6), 1, keepdims=True)
    hi = jnp.max(jnp.where(same, lanef, -1.0), 1, keepdims=True)
    locb = jnp.broadcast_to(local, (128, 128)) + 1.0
    id0 = jnp.sum(jnp.where(lanef == lo, locb, 0.0), 1, keepdims=True) - 1.0
    id1 = jnp.sum(jnp.where((lanef == hi) & (hi > lo), locb, 0.0), 1, keepdims=True) - 1.0
    some = jnp.maximum(hi, 0.0)
    row = jnp.where(lane == 0, id0, jnp.where(lane == 1, id1, jnp.where(lane == 2, jnp.minimum(lo, some), jnp.where(
        lane == 3, some, jnp.where(lane == 4, jnp.maximum(id0, 0.0), jnp.maximum(id1, 0.0))))))
    req_ref[:, 0, :] = row.astype(i32)
    ownc = spread(owner)
    before = jnp.where((ownc == jnp.broadcast_to(owner, (128, 128))) & (sub < lane), 1.0, 0.0)
    second = jnp.sum(before, 0, keepdims=True)
    out = jnp.concatenate([owner * 9.0 + second * 4.0, second, owner * 9.0 + 8.0, owner], 0)
    slot_ref[...] = out.astype(i32)


def make_requests(support):
    return pl.pallas_call(
        request_kernel,
        out_shape=(jax.ShapeDtypeStruct((128, 1, 128), i32), jax.ShapeDtypeStruct((4, 128), i32)),
        in_specs=[VMEM], out_specs=(VMEM, VMEM), name="make_requests",
    )(support.reshape(1, 128))


def lookup(tab, idx):
    low = idx & 127
    high = idx >> 7
    out = jnp.zeros((8, 128), f32)
    for r in range(32):
        got = jnp.take_along_axis(jnp.broadcast_to(tab[r:r + 1, :], (8, 128)), low, axis=1)
        out = jnp.where(high == r, got, out)
    return out


def fine_kernel(slot_ref, req_ref, ftab_ref, gtab_ref, src_ref, sclu_ref, tile_ref, oclu_ref, inc_ref,
                cf_ref, cg_ref, ff_ref, fg_ref,
                gs, fs, sg, ccl, xt0, xt1, fx0, fx1, sc0, sc1, rm0, rm1, sa, lse, back, ret, idr, mt, ex,
                ssem, rsem, lsem):
    row = lax.axis_index("row")
    col = lax.axis_index("col")
    me = row * 32 + col
    barrier = pltpu.get_barrier_semaphore()
    each(DEV - 1, lambda d: pl.semaphore_signal(barrier, inc=1, device_id=place(lax.rem(me + d + 1, DEV)),
                                                device_id_type=MESH))
    cf_ref[...] = ftab_ref[pl.ds(pl.multiple_of(row * 8, 8), 8), :]
    cg_ref[...] = gtab_ref[pl.ds(col, 1), :]
    ft = ftab_ref[...] * KAPPA
    gt = gtab_ref[...] * KAPPA

    def clusters(e):
        both = tile_ref[slot_ref[2, e]]
        second = slot_ref[1, e].astype(f32) > 0.5
        ccl[e] = jnp.where(second, both[2:4], both[0:2])

    each(DEV, clusters)
    for r in range(2):
        fs[block(r, 8), :] = lookup(ft, sclu_ref[block(r, 8), :])

    def own(r):
        rows = pl.ds(pl.multiple_of(r * 8, 8), 8)
        sg[rows, :] = lookup(gt, oclu_ref[rows, :])

    each(8, own)

    def sent(r):
        rows = pl.ds(pl.multiple_of(r * 4, 4), 4)
        gs[rows, :, :] = lookup(gt, ccl[rows, :, :].reshape(8, 128).astype(i32)).reshape(4, 2, 128)

    each(32, sent)

    def left(b, xt, fx):
        for h in range(2):
            xt[block(h), :] = left_rows(src_ref[:, pl.ds(pl.multiple_of(b * BLK + h * 128, 128), 128)])
            fx[block(h), :] = spread(fs[pl.ds(2 * b + h, 1), :])

    def duals(e):
        return [gs[e, h:h + 1, :] for h in range(2)]

    def product(b, k, xt, sc, rm):
        e = b * SUPP + k
        i = slot_ref[0, e]
        part = [jnp.concatenate([tile_ref[i + 2 * h], tile_ref[i + 2 * h + 1]], 0) for h in range(2)]
        y = jnp.concatenate(part, 1)
        st = stack(y, jnp.concatenate(duals(e), 1) - KAPPA * jnp.sum(y * y, 0, keepdims=True), False)
        d = jnp.dot(xt[...], st, preferred_element_type=f32)
        sc[k] = d
        rm[...] = jnp.maximum(rm[...], jnp.maximum(d[:, :128], d[:, 128:]))

    def col_part(b, k, sc, fx):
        g = duals(b * SUPP + k)
        for h in range(2):
            v = sc[k, :, block(h)] + fx[...]
            m = jnp.max(v, 0, keepdims=True)
            s = jnp.sum(jnp.exp2(v - m), 0, keepdims=True)
            lse[b * SUPP + k, h:h + 1, :] = m + jnp.log2(s) - g[h]

    def row_part(k, sc, rm):
        m = rm[...]
        return jnp.exp2(sc[k, :, :128] - m) + jnp.exp2(sc[k, :, 128:] - m)

    def one(b, xt, fx, sc, rm, prev):
        left(b, xt, fx)
        rm[...] = jnp.full_like(rm, -jnp.inf)
        product(b, 0, xt, sc, rm)
        product(b, 1, xt, sc, rm)
        if prev is not None:
            sa[...] = jnp.zeros_like(sa)

        def some(g):
            if prev is not None:
                sa[...] = sa[...] + row_part(2 * g, *prev) + row_part(2 * g + 1, *prev)
            for u in range(2):
                col_part(b, 2 * g + u, sc, fx)
            for u in range(2):
                product(b, lax.rem(2 * g + 2 + u, SUPP), xt, sc, rm)

        each(SUPP // 2, some)
        rm[...] = jnp.broadcast_to(jnp.max(rm[...], 1, keepdims=True), (BLK, 128))
        if prev is not None:
            finish(b - 1, prev[1])

    def finish(b, rm):
        out = rm[...] + jnp.log2(jnp.sum(sa[...], 1, keepdims=True)) - math.log2(SUPP * BLK)
        for h in range(2):
            ff_ref[pl.ds(2 * b + h, 1), :] = (0.5 * UNIT) * (fs[pl.ds(2 * b + h, 1), :] - out[block(h), :].T[:1, :])

    one(0, xt0, fx0, sc0, rm0, None)

    def two(p):
        one(2 * p + 1, xt1, fx1, sc1, rm1, (sc0, rm0))
        one(2 * p + 2, xt0, fx0, sc0, rm0, (sc1, rm1))

    each(3, two)
    one(7, xt1, fx1, sc1, rm1, (sc0, rm0))

    def fill(p):
        for q in range(2):
            back[p, 2 * q:2 * q + 2, :] = lse[req_ref[p, 0, 2 + q]]

    each(DEV, fill)

    def ret_copy(d):
        to = lax.rem(me + d + 1, DEV)
        return remote(back.at[to], ret.at[me], ssem.at[d], rsem.at[d], place(to))

    pl.semaphore_wait(barrier, DEV - 1)
    each(DEV - 1, lambda d: ret_copy(d).start())
    mine = pltpu.make_async_copy(back.at[me], ret.at[me], lsem)
    mine.start()
    sa[...] = jnp.zeros_like(sa)

    def last(k):
        sa[...] = sa[...] + row_part(k, sc1, rm1)

    each(SUPP, last)
    finish(7, rm1)
    lane = lax.broadcasted_iota(i32, (DEV, 128), 1).astype(f32)
    sub = lax.broadcasted_iota(i32, (DEV, 128), 0).astype(f32)
    hot, hot_t = [], []
    for q in range(2):
        idv = jnp.broadcast_to(inc_ref[:, 0, q:q + 1].astype(f32), (DEV, 128))
        idr[q] = idv
        hot.append(jnp.where(idv == lane, 1.0, 0.0).astype(bf16))
        hot_t.append(jnp.where(idv.T == sub, 1.0, 0.0).astype(bf16))
    count = sum(jnp.sum(h.astype(f32), 1, keepdims=True) for h in hot_t)
    mt[...] = jnp.zeros_like(mt)
    mine.wait()
    each(DEV - 1, lambda d: ret_copy(d).wait())
    for q in range(2):
        for h in range(2):
            ex[q, h] = ret[:, 2 * q + h, :]

    def tops(t):
        tf = t.astype(f32)
        for h in range(2):
            m = jnp.maximum(jnp.where(idr[0] == tf, ex[0, h], -jnp.inf), jnp.where(idr[1] == tf, ex[1, h], -jnp.inf))
            mt[h, pl.ds(t, 1), :] = jnp.max(m, 0, keepdims=True)

    each(TB_DEV, tops)
    for h in range(2):
        tot = jnp.zeros((DEV, 128), f32)
        mparts = split3(mt[h])
        for q in range(2):
            mx = sum(jnp.dot(hot[q], mp, preferred_element_type=f32) for mp in mparts)
            e = jnp.where(idr[q] >= 0.0, jnp.exp2(ex[q, h] - mx), 0.0)
            tot = tot + sum(jnp.dot(hot_t[q], ep, preferred_element_type=f32) for ep in split3(e))
        ex[0, h] = mt[h] + jnp.log2(tot) - jnp.log2(jnp.broadcast_to(count, (DEV, 128)) * BLK)
    for t in range(TB_DEV):
        for h in range(2):
            fg_ref[2 * t + h:2 * t + h + 1, :] = (0.5 * UNIT) * (sg[2 * t + h:2 * t + h + 1, :] - ex[0, h, t:t + 1, :])


def fine(slots, req, ftab, gtab, src_pts, src_cluster, tiles, tgt_cluster, incoming):
    S = jax.ShapeDtypeStruct
    V = pltpu.VMEM
    dma = pltpu.SemaphoreType.DMA
    return pl.pallas_call(
        fine_kernel,
        out_shape=(S((8, 128), f32), S((1, 128), f32), S((16, 128), f32), S((64, 128), f32)),
        in_specs=[SMEM, SMEM] + [VMEM] * 7,
        out_specs=(VMEM,) * 4,
        scratch_shapes=[V((DEV, 2, 128), f32), V((16, 128), f32), V((64, 128), f32), V((DEV, 2, 128), f32),
                        V((BLK, 128), bf16), V((BLK, 128), bf16), V((BLK, 128), f32), V((BLK, 128), f32),
                        V((SUPP, BLK, BLK), f32), V((SUPP, BLK, BLK), f32), V((BLK, 128), f32), V((BLK, 128), f32),
                        V((BLK, 128), f32), V((DEV, 2, 128), f32), V((DEV, 4, 128), f32), V((DEV, 4, 128), f32),
                        V((2, DEV, 128), f32), V((2, DEV, 128), f32), V((2, 2, DEV, 128), f32),
                        dma((DEV,)), dma((DEV,)), dma],
        compiler_params=pltpu.CompilerParams(collective_id=2, has_side_effects=True,
                                             vmem_limit_bytes=48 * 1024 * 1024),
        name="fine",
    )(slots, req, ftab, gtab, src_pts, src_cluster.reshape(16, 128), tiles.reshape(DEV * 9, 8, 128), tgt_cluster.reshape(64, 128), incoming)


def on_device(src_cent, tgt_cent, src_mass, tgt_mass, src_pts, tgt_pts, src_cluster, tgt_cluster, support):
    req, slots = make_requests(support)
    ftab, gtab, tiles, incoming = coarse(src_cent, src_mass, tgt_cent, tgt_mass, req, tgt_pts, tgt_cluster)
    cf, cg, ff, fg = fine(slots, req, ftab, gtab, src_pts, src_cluster, tiles, tgt_cluster, incoming)
    return cf.reshape(-1), cg.reshape(-1), ff.reshape(-1), fg.reshape(-1)


def solution(mesh):
    both = ("row", "col")
    in_specs = (P(None, "row"), P(None, "col"), P("row"), P("col"), P(None, both), P(None, both), P(both), P(both),
                P(both, None))
    out_specs = (P("row"), P("col"), P(both), P(both))
    return jax.shard_map(on_device, mesh=mesh, in_specs=in_specs, out_specs=out_specs, check_vma=False)
```

```python
import math

import jax
import jax.numpy as jnp
from jax import lax
from jax.experimental import pallas as pl
from jax.experimental.pallas import tpu as pltpu
from jax.sharding import PartitionSpec as P

MESH = pl.DeviceIdType.MESH
F = 16
BLK = 256
SUPP = 16
SB_DEV = 8
TB_DEV = 32
KS = 4096
KT = 4096
EPS = 0.1
KAPPA = math.log2(math.e) / EPS
UNIT = EPS * math.log(2.0)
DEV = 128
STRIDE = 37
UNR = 4
PART = KS // 4
CH = 64
NJ = KT // 128
VMEM = pl.BlockSpec(memory_space=pltpu.VMEM)
SMEM = pl.BlockSpec(memory_space=pltpu.SMEM)
f32 = jnp.float32
i32 = jnp.int32
bf16 = jnp.bfloat16


def split3(v):
    hi = v.astype(bf16)
    rest = v - hi.astype(f32)
    mid = rest.astype(bf16)
    return hi, mid, (rest - mid.astype(f32)).astype(bf16)


def stack(pts, term, left):
    h, m, l = split3(pts)
    n = pts.shape[1]
    th, tm, tl = [v.astype(f32) for v in split3(term)]
    rid = lax.broadcasted_iota(i32, (16, n), 0)
    base, ones = (0, 3) if left else (3, 0)
    extra = jnp.where(rid == base, th, jnp.where(rid == base + 1, tm, jnp.where(rid == base + 2, tl, 0.0)))
    extra = jnp.where((rid >= ones) & (rid < ones + 3), 1.0, extra).astype(bf16)
    zero = jnp.zeros((16, n), bf16)
    if left:
        return jnp.concatenate([h, h, m, h, l, m, extra, zero], 0)
    return jnp.concatenate([h, m, h, l, h, m, extra, zero], 0)


def left_rows(x, dual=0.0):
    term = dual - KAPPA * jnp.sum(x * x, 0, keepdims=True)
    return stack((2.0 * KAPPA) * x, term, True).astype(f32).T.astype(bf16)


def spread(row):
    return jnp.broadcast_to(row, (128, 128)).T


def block(j, width=128):
    return slice(j * width, (j + 1) * width)


def place(index):
    return {"row": lax.div(index, 32), "col": lax.rem(index, 32)}


def remote(src, dst, ssem, rsem, where):
    return pltpu.make_async_remote_copy(src_ref=src, dst_ref=dst, send_sem=ssem, recv_sem=rsem, device_id=where,
                                        device_id_type=MESH)


def each(n, body):
    def step(i, c):
        body(i)
        return c

    lax.fori_loop(0, n, step, 0)


def coarse_kernel(src_in, smass_in, tgt_in, tmass_in, req_ref, pts_ref, clu_ref,
                  ftab_ref, gtab_ref, tiles_ref, inc_ref,
                  src_all, smass_all, tgt_all, tmass_all, inc_s, blocks, out_buf,
                  a_scr, t0, t1, ys, xs, gp, lb, acc, fst, am, sh, mxs, rs, rbuf, fbuf,
                  send_sem, recv_sem, cs_sem, cr_sem, qs_sem, qr_sem, bs_sem, br_sem, lsem):
    row = lax.axis_index("row")
    col = lax.axis_index("col")
    me = row * 32 + col
    core = lax.rem(col, 2)
    quarter = lax.rem(row, 2) * 2 + core
    barrier = pltpu.get_barrier_semaphore()
    each(DEV - 1, lambda d: pl.semaphore_signal(barrier, inc=1, device_id=place(lax.rem(me + d + 1, DEV)),
                                                device_id_type=MESH))

    def quarter_of(r):
        return pl.ds(pl.multiple_of((lax.rem(r, 2) * 2 + core) * 256, 256), 256)


    def tgt_copy(d, a):
        where = {"row": row, "col": lax.rem(col + d + 1, 32)}
        src, dst = ((tgt_in, tgt_all), (tmass_in, tmass_all))[a]
        return remote(src, dst.at[col], cs_sem.at[d, a], cr_sem.at[d, a], where)

    def src_copy(d, a):
        to = lax.rem(row + d + 1, 4)
        src, dst = ((src_in, src_all), (smass_in, smass_all))[a]
        return remote(src.at[:, quarter_of(to)], dst.at[row], cs_sem.at[31 + d, a], cr_sem.at[31 + d, a],
                      {"row": to, "col": col})

    def req_copy(d):
        to = lax.rem(me + d + 1, DEV)
        return remote(req_ref.at[to], inc_ref.at[me], qs_sem.at[d], qr_sem.at[d], place(to))

    def blk_copy(d):
        to = lax.rem(me + lax.rem((d + 1) * STRIDE, DEV), DEV)
        return remote(out_buf.at[to], tiles_ref.at[me], bs_sem.at[d], br_sem.at[d], place(to))

    local = [pltpu.make_async_copy(tgt_in, tgt_all.at[col], lsem.at[0]),
             pltpu.make_async_copy(tmass_in, tmass_all.at[col], lsem.at[1]),
             pltpu.make_async_copy(src_in.at[:, quarter_of(row)], src_all.at[row], lsem.at[2]),
             pltpu.make_async_copy(smass_in.at[:, quarter_of(row)], smass_all.at[row], lsem.at[3]),
             pltpu.make_async_copy(req_ref.at[me], inc_ref.at[me], lsem.at[4])]
    for c in local:
        c.start()
    pl.semaphore_wait(barrier, DEV - 1)

    def start_src(d):
        src_copy(d, 0).start()
        src_copy(d, 1).start()

    def start_tgt(d):
        tgt_copy(d, 0).start()
        tgt_copy(d, 1).start()

    def wait_src(d):
        src_copy(d, 0).wait()
        src_copy(d, 1).wait()

    def wait_tgt(d):
        tgt_copy(d, 0).wait()
        tgt_copy(d, 1).wait()

    each(3, start_src)
    each(31, start_tgt)
    each(DEV - 1, lambda d: req_copy(d).start())
    for c in local:
        c.wait()
    each(3, wait_src)
    each(31, wait_tgt)
    for k in range(32):
        y = tgt_all[k]
        lbk = jnp.log2(tmass_all[k])
        ys[:, block(k)] = stack(y, lbk - KAPPA * jnp.sum(y * y, 0, keepdims=True), False)
        lb[:, block(k)] = jnp.broadcast_to(lbk, (8, 128))
    for q in range(4):
        for h in range(2):
            r0 = q * 256 + h * 128
            xs[r0:r0 + 128, :] = left_rows(src_all[q, :, block(h)])
            am[r0:r0 + 128, :] = spread(smass_all[q, :, block(h)])

    for t in range(TB_DEV):
        for h in range(2):
            blocks[t, h * 16:h * 16 + 16, :] = pts_ref[:, block(2 * t + h)]
    each(DEV - 1, lambda d: req_copy(d).wait())
    to_scalar = pltpu.make_async_copy(inc_ref, inc_s, lsem.at[5])
    to_scalar.start()
    to_scalar.wait()

    def fill(p):
        for q in range(2):
            t = inc_s[p, 0, 4 + q]
            out_buf[p, q * 32:q * 32 + 32, :] = blocks[t]
            out_buf[p, 64 + 2 * q:66 + 2 * q, :] = clu_ref[t].astype(f32)
        out_buf[p, 68:72, :] = jnp.zeros((4, 128), f32)

    each(DEV, fill)
    each(43, lambda d: blk_copy(d).start())
    own = pltpu.make_async_copy(out_buf.at[me], tiles_ref.at[me], lsem.at[6])
    own.start()

    acc[...] = jnp.full_like(acc, -jnp.inf)

    def rows_of(n):
        return pl.ds(pl.multiple_of(n * CH, CH), CH)

    def first(b):
        wide = pl.ds(pl.multiple_of(b * 256, 256), 256)
        mx = jnp.full((256, 128), -jnp.inf, f32)
        for c in range(NJ // 2):
            d = jnp.dot(xs[wide, :], ys[:, block(c, 256)], preferred_element_type=f32)
            a_scr[wide, block(c, 256)] = d
            mx = jnp.maximum(mx, jnp.maximum(d[:, :128], d[:, 128:]))
        mxs[...] = jnp.broadcast_to(jnp.max(mx, 1, keepdims=True), (256, 128))
        fl = None
        for q in range(5):
            now, prev = rows_of(4 * b + q), rows_of(4 * b + q - 1)
            s = None
            for j in range(NJ):
                if q < 4:
                    e = jnp.exp2(a_scr[now, block(j)] - mxs[block(q, CH), :])
                    s = e if s is None else s + e
                if q > 0:
                    v = a_scr[prev, block(j)] + fl
                    acc[:, block(j)] = jnp.maximum(acc[:, block(j)], jnp.max(v.reshape(CH // 8, 8, 128), 0))
            if q < 4:
                f1 = -(mxs[block(q, CH), :] + jnp.log2(jnp.broadcast_to(jnp.sum(s, 1, keepdims=True), (CH, 128))))
                fst[now, :] = f1
                fl = f1 + jnp.log2(am[now, :])

    each(PART // 256, first)
    for j in range(NJ):
        gp[:, block(j)] = jnp.broadcast_to(jnp.max(acc[:, block(j)], 0, keepdims=True), (8, 128))
    acc[...] = jnp.zeros_like(acc)

    def second(c):
        fl = fst[rows_of(c), :] + jnp.log2(am[rows_of(c), :])
        for j in range(NJ):
            v = a_scr[rows_of(c), block(j)] + fl
            a_scr[rows_of(c), block(j)] = v
            v = jnp.exp2(v.reshape(CH // 8, 8, 128) - gp[:, block(j)][None])
            acc[:, block(j)] = acc[:, block(j)] + jnp.sum(v, 0)

    each(PART // CH, second)
    for j in range(NJ):
        rbuf[0, quarter, :, block(j)] = gp[:1, block(j)] + jnp.log2(jnp.sum(acc[:, block(j)], 0, keepdims=True))

    def to_group(buf, k):
        out = []
        for d in range(3):
            to = lax.rem(quarter + d + 1, 4)
            where = {"row": row - lax.rem(row, 2) + lax.div(to, 2), "col": col - core + lax.rem(to, 2)}
            out.append(remote(buf, buf, send_sem.at[k, d], recv_sem.at[k, d], where))
        return out

    def swap(k, send=True):
        copies = to_group(rbuf.at[k, quarter], k)
        for c in copies:
            c.start()
        if send:
            each(12, lambda d: blk_copy(43 + 12 * k + d).start())
        for c in copies:
            c.wait()

    swap(0)
    for j in range(NJ):
        ls = [rbuf[0, i, :, block(j)] for i in range(4)]
        m = jnp.maximum(jnp.maximum(ls[0], ls[1]), jnp.maximum(ls[2], ls[3]))
        l = m + jnp.log2(sum(jnp.exp2(v - m) for v in ls))
        gp[:, block(j)] = lb[:, block(j)] - jnp.broadcast_to(l, (8, 128))

    def turn(k, renew=False, send=True):
        acc[...] = jnp.zeros_like(acc)

        def both(tn, n, tp, p):
            if tp is not None:
                rows = rows_of(p)
                u = am[rows, :] / jnp.broadcast_to(jnp.sum(rs[...], 1, keepdims=True), (CH, 128))
                sh[rows, :] = -jnp.log2(u)
            if tn is not None:
                rows = rows_of(n)
                if renew:
                    move = sh[rows, :]
                    fst[rows, :] = fst[rows, :] - move
            r = None
            for j in range(NJ):
                if tn is not None:
                    v = a_scr[rows, block(j)]
                    if renew:
                        v = v - move
                        a_scr[rows, block(j)] = v
                    e = jnp.exp2(v.reshape(CH // 8, 8, 128) + gp[:, block(j)][None]).reshape(CH, 128)
                    tn[:, block(j)] = e
                    r = e if r is None else r + e
                if tp is not None:
                    v = (tp[:, block(j)] * u).reshape(CH // 8, 8, 128)
                    acc[:, block(j)] = acc[:, block(j)] + jnp.sum(v, 0)
            if tn is not None:
                rs[...] = r

        def chunk(c):
            both(t1, 2 * c + 1, t0, 2 * c)
            both(t0, 2 * c + 2, t1, 2 * c + 1)

        last = PART // CH - 1
        both(t0, 0, None, None)
        each(last // 2, chunk)
        both(t1, last, t0, last - 1)
        both(None, None, t1, last)
        for j in range(NJ):
            rbuf[k, quarter, :, block(j)] = jnp.sum(acc[:, block(j)], 0, keepdims=True)
        swap(k, send)
        for j in range(NJ):
            c = jnp.broadcast_to(sum(rbuf[k, i, :, block(j)] for i in range(4)), (8, 128))
            gp[:, block(j)] = gp[:, block(j)] + (lb[:, block(j)] - jnp.log2(c))

    each(3, lambda i: turn(i + 1))
    turn(4, renew=True)
    each(2, lambda i: turn(i + 5))
    turn(7, send=False)
    for h in range(8):
        fbuf[quarter, h:h + 1, :] = ((fst[block(h), :] - sh[block(h), :]) * UNIT).T[:1, :]
    copies = to_group(fbuf.at[quarter], 8)
    for c in copies:
        c.start()
    for j in range(NJ):
        gtab_ref[j:j + 1, :] = gp[:1, block(j)] * UNIT
    for c in copies:
        c.wait()
    for q in range(4):
        for i in range(4):
            ftab_ref[q * 8 + 2 * i:q * 8 + 2 * i + 2, :] = fbuf[i, 2 * q:2 * q + 2, :]
    own.wait()
    each(DEV - 1, lambda d: blk_copy(d).wait())


def coarse(src_cent, src_mass, tgt_cent, tgt_mass, req, tgt_pts, tgt_cluster):
    V = pltpu.VMEM
    S = jax.ShapeDtypeStruct
    dma = pltpu.SemaphoreType.DMA
    return pl.pallas_call(
        coarse_kernel,
        out_shape=(S((32, 128), f32), S((32, 128), f32), S((DEV, 72, 128), f32), S((DEV, 1, 128), i32)),
        in_specs=[VMEM] * 7,
        out_specs=(VMEM, VMEM, pl.BlockSpec(memory_space=pl.ANY), VMEM),
        scratch_shapes=[V((4, F, 256), f32), V((4, 1, 256), f32), V((32, F, 128), f32), V((32, 1, 128), f32),
                        pltpu.SMEM((DEV, 1, 128), i32), V((TB_DEV, 32, 128), f32), V((DEV, 72, 128), f32),
                        V((PART, KT), f32), V((CH, KT), f32), V((CH, KT), f32),
                        V((128, KT), bf16), V((PART, 128), bf16), V((8, KT), f32), V((8, KT), f32), V((8, KT), f32),
                        V((PART, 128), f32), V((PART, 128), f32), V((PART, 128), f32), V((256, 128), f32), V((CH, 128), f32),
                        V((8, 4, 1, KT), f32), V((4, 8, 128), f32),
                        dma((9, 3)), dma((9, 3)),
                        dma((34, 2)), dma((34, 2)), dma((DEV,)), dma((DEV,)), dma((DEV,)), dma((DEV,)), dma((7,))],
        compiler_params=pltpu.CompilerParams(collective_id=1, has_side_effects=True,
                                             vmem_limit_bytes=62 * 1024 * 1024),
        name="coarse",
    )(src_cent, src_mass.reshape(1, -1), tgt_cent, tgt_mass.reshape(1, -1), req, tgt_pts,
      tgt_cluster.reshape(TB_DEV, 2, 128))


def request_kernel(sup_ref, req_ref, slot_ref):
    wanted = sup_ref[...].astype(f32)
    owner = jnp.floor(wanted * (1.0 / TB_DEV))
    local = wanted - owner * TB_DEV
    sub = lax.broadcasted_iota(i32, (128, 128), 0)
    lane = lax.broadcasted_iota(i32, (128, 128), 1)
    lanef = lane.astype(f32)
    same = jnp.broadcast_to(owner, (128, 128)) == sub.astype(f32)
    lo = jnp.min(jnp.where(same, lanef, 1e6), 1, keepdims=True)
    hi = jnp.max(jnp.where(same, lanef, -1.0), 1, keepdims=True)
    locb = jnp.broadcast_to(local, (128, 128)) + 1.0
    id0 = jnp.sum(jnp.where(lanef == lo, locb, 0.0), 1, keepdims=True) - 1.0
    id1 = jnp.sum(jnp.where((lanef == hi) & (hi > lo), locb, 0.0), 1, keepdims=True) - 1.0
    some = jnp.maximum(hi, 0.0)
    row = jnp.where(lane == 0, id0, jnp.where(lane == 1, id1, jnp.where(lane == 2, jnp.minimum(lo, some), jnp.where(
        lane == 3, some, jnp.where(lane == 4, jnp.maximum(id0, 0.0), jnp.maximum(id1, 0.0))))))
    req_ref[:, 0, :] = row.astype(i32)
    ownc = spread(owner)
    before = jnp.where((ownc == jnp.broadcast_to(owner, (128, 128))) & (sub < lane), 1.0, 0.0)
    second = jnp.sum(before, 0, keepdims=True)
    out = jnp.concatenate([owner * 9.0 + second * 4.0, second, owner * 9.0 + 8.0, owner], 0)
    slot_ref[...] = out.astype(i32)


def make_requests(support):
    return pl.pallas_call(
        request_kernel,
        out_shape=(jax.ShapeDtypeStruct((128, 1, 128), i32), jax.ShapeDtypeStruct((4, 128), i32)),
        in_specs=[VMEM], out_specs=(VMEM, VMEM), name="make_requests",
    )(support.reshape(1, 128))


def lookup(tab, idx):
    low = idx & 127
    high = idx >> 7
    out = jnp.zeros((8, 128), f32)
    for r in range(32):
        got = jnp.take_along_axis(jnp.broadcast_to(tab[r:r + 1, :], (8, 128)), low, axis=1)
        out = jnp.where(high == r, got, out)
    return out


def fine_kernel(slot_ref, req_ref, ftab_ref, gtab_ref, src_ref, sclu_ref, tile_hbm, oclu_ref, inc_ref,
                cf_ref, cg_ref, ff_ref, fg_ref,
                tile_ref, gs, fs, sg, ccl, xt0, xt1, cm, sc0, sc1, rm0, rm1, sa, lse, back, ret, idr, mt, ex,
                ssem, rsem, lsem, tsem):
    fetch = pltpu.make_async_copy(tile_hbm, tile_ref, tsem)
    fetch.start()
    row = lax.axis_index("row")
    col = lax.axis_index("col")
    me = row * 32 + col
    barrier = pltpu.get_barrier_semaphore()
    each(DEV - 1, lambda d: pl.semaphore_signal(barrier, inc=1, device_id=place(lax.rem(me + d + 1, DEV)),
                                                device_id_type=MESH))
    cf_ref[...] = ftab_ref[pl.ds(pl.multiple_of(row * 8, 8), 8), :]
    cg_ref[...] = gtab_ref[pl.ds(col, 1), :]
    ft = ftab_ref[...] * KAPPA
    gt = gtab_ref[...] * KAPPA

    def clusters(e):
        both = tile_ref[slot_ref[2, e]]
        second = slot_ref[1, e].astype(f32) > 0.5
        ccl[pl.ds(2 * e, 2), :] = jnp.where(second, both[2:4], both[0:2])

    for r in range(2):
        fs[block(r, 8), :] = lookup(ft, sclu_ref[block(r, 8), :])

    def own(r):
        rows = pl.ds(pl.multiple_of(r * 8, 8), 8)
        sg[rows, :] = lookup(gt, oclu_ref[rows, :])

    each(8, own)
    fetch.wait()
    each(DEV, clusters)

    def sent(r):
        rows = pl.ds(pl.multiple_of(r * 8, 8), 8)
        gs[rows, :] = lookup(gt, ccl[rows, :].astype(i32))

    each(32, sent)

    def left(b, xt):
        for h in range(2):
            x = src_ref[:, pl.ds(pl.multiple_of(b * BLK + h * 128, 128), 128)]
            xt[block(h), :] = left_rows(x, fs[pl.ds(2 * b + h, 1), :])

    def duals(e):
        return [gs[pl.ds(2 * e + h, 1), :] for h in range(2)]

    def product(b, k, xt, sc, rm, cm):
        e = b * SUPP + k
        i = slot_ref[0, e]
        part = [jnp.concatenate([tile_ref[i + 2 * h], tile_ref[i + 2 * h + 1]], 0) for h in range(2)]
        y = jnp.concatenate(part, 1)
        st = stack(y, jnp.concatenate(duals(e), 1) - KAPPA * jnp.sum(y * y, 0, keepdims=True), False)
        d = jnp.dot(xt[...], st, preferred_element_type=f32)
        sc[k] = d
        rm[...] = jnp.maximum(rm[...], jnp.maximum(d[:, :128], d[:, 128:]))
        cm[k] = jnp.broadcast_to(jnp.max(d, 0, keepdims=True), (8, BLK))

    def col_part(b, k, sc, cm):
        g = duals(b * SUPP + k)
        for h in range(2):
            m = cm[k, :, block(h)]
            s = jnp.sum(jnp.exp2(sc[k, :, block(h)].reshape(BLK // 8, 8, 128) - m[None]), 0)
            lse[b * SUPP + k, h:h + 1, :] = m[:1] + jnp.log2(jnp.sum(s, 0, keepdims=True)) - g[h]

    def row_part(ks, sc, rm):
        for r in range(BLK // 64):
            m = rm[block(r, 64), :]
            s = sa[block(r, 64), :]
            for k in ks:
                s = s + (jnp.exp2(sc[k, block(r, 64), :128] - m) + jnp.exp2(sc[k, block(r, 64), 128:] - m))
            sa[block(r, 64), :] = s

    def one(b, xt, sc, rm, prev):
        left(b, xt)
        rm[...] = jnp.full_like(rm, -jnp.inf)
        for u in range(UNR):
            product(b, u, xt, sc, rm, cm)
        if prev is not None:
            sa[...] = jnp.zeros_like(sa)

        def some(g):
            for u in range(UNR):
                col_part(b, UNR * g + u, sc, cm)
            if prev is not None:
                row_part([UNR * g + u for u in range(UNR)], *prev)
            for u in range(UNR):
                product(b, lax.rem(UNR * g + UNR + u, SUPP), xt, sc, rm, cm)

        each(SUPP // UNR, some)
        rm[...] = jnp.broadcast_to(jnp.max(rm[...], 1, keepdims=True), (BLK, 128))
        if prev is not None:
            finish(b - 1, prev[1])

    def finish(b, rm):
        out = rm[...] + jnp.log2(jnp.sum(sa[...], 1, keepdims=True)) - math.log2(SUPP * BLK)
        for h in range(2):
            mine = fs[pl.ds(2 * b + h, 1), :]
            ff_ref[pl.ds(2 * b + h, 1), :] = (0.5 * UNIT) * (mine - (out[block(h), :].T[:1, :] - mine))

    one(0, xt0, sc0, rm0, None)

    def two(p):
        one(2 * p + 1, xt1, sc1, rm1, (sc0, rm0))
        one(2 * p + 2, xt0, sc0, rm0, (sc1, rm1))

    each(3, two)
    one(7, xt1, sc1, rm1, (sc0, rm0))

    def fill(p):
        for q in range(2):
            back[p, 2 * q:2 * q + 2, :] = lse[req_ref[p, 0, 2 + q]]

    each(DEV, fill)

    def ret_copy(d):
        to = lax.rem(me + d + 1, DEV)
        return remote(back.at[to], ret.at[me], ssem.at[d], rsem.at[d], place(to))

    pl.semaphore_wait(barrier, DEV - 1)
    each(DEV - 1, lambda d: ret_copy(d).start())
    mine = pltpu.make_async_copy(back.at[me], ret.at[me], lsem)
    mine.start()
    sa[...] = jnp.zeros_like(sa)

    each(SUPP // 2, lambda g: row_part((2 * g, 2 * g + 1), sc1, rm1))
    finish(7, rm1)
    lane = lax.broadcasted_iota(i32, (DEV, 128), 1).astype(f32)
    sub = lax.broadcasted_iota(i32, (DEV, 128), 0).astype(f32)
    hot, hot_t = [], []
    for q in range(2):
        idv = jnp.broadcast_to(inc_ref[:, 0, q:q + 1].astype(f32), (DEV, 128))
        idr[q] = idv
        hot.append(jnp.where(idv == lane, 1.0, 0.0).astype(bf16))
        hot_t.append(jnp.where(idv.T == sub, 1.0, 0.0).astype(bf16))
    count = sum(jnp.sum(h.astype(f32), 1, keepdims=True) for h in hot_t)
    mt[...] = jnp.zeros_like(mt)
    mine.wait()
    each(DEV - 1, lambda d: ret_copy(d).wait())
    for q in range(2):
        for h in range(2):
            ex[q, h] = ret[:, 2 * q + h, :]

    def tops(t):
        tf = t.astype(f32)
        for h in range(2):
            m = jnp.maximum(jnp.where(idr[0] == tf, ex[0, h], -jnp.inf), jnp.where(idr[1] == tf, ex[1, h], -jnp.inf))
            mt[h, pl.ds(t, 1), :] = jnp.max(m, 0, keepdims=True)

    each(TB_DEV, tops)
    for h in range(2):
        tot = jnp.zeros((DEV, 128), f32)
        mparts = split3(mt[h])
        for q in range(2):
            mx = sum(jnp.dot(hot[q], mp, preferred_element_type=f32) for mp in mparts)
            e = jnp.where(idr[q] >= 0.0, jnp.exp2(ex[q, h] - mx), 0.0)
            tot = tot + sum(jnp.dot(hot_t[q], ep, preferred_element_type=f32) for ep in split3(e))
        ex[0, h] = mt[h] + jnp.log2(tot) - jnp.log2(jnp.broadcast_to(count, (DEV, 128)) * BLK)
    for t in range(TB_DEV):
        for h in range(2):
            fg_ref[2 * t + h:2 * t + h + 1, :] = (0.5 * UNIT) * (sg[2 * t + h:2 * t + h + 1, :] - ex[0, h, t:t + 1, :])


def fine(slots, req, ftab, gtab, src_pts, src_cluster, tiles, tgt_cluster, incoming):
    S = jax.ShapeDtypeStruct
    V = pltpu.VMEM
    dma = pltpu.SemaphoreType.DMA
    return pl.pallas_call(
        fine_kernel,
        out_shape=(S((8, 128), f32), S((1, 128), f32), S((16, 128), f32), S((64, 128), f32)),
        in_specs=[SMEM, SMEM] + [VMEM] * 4 + [pl.BlockSpec(memory_space=pl.ANY)] + [VMEM] * 2,
        out_specs=(VMEM,) * 4,
        scratch_shapes=[V((DEV * 9, 8, 128), f32), V((2 * DEV, 128), f32), V((16, 128), f32), V((64, 128), f32),
                        V((2 * DEV, 128), f32), V((BLK, 128), bf16), V((BLK, 128), bf16), V((SUPP, 8, BLK), f32),
                        V((SUPP, BLK, BLK), f32), V((SUPP, BLK, BLK), f32), V((BLK, 128), f32), V((BLK, 128), f32),
                        V((BLK, 128), f32), V((DEV, 2, 128), f32), V((DEV, 4, 128), f32), V((DEV, 4, 128), f32),
                        V((2, DEV, 128), f32), V((2, DEV, 128), f32), V((2, 2, DEV, 128), f32),
                        dma((DEV,)), dma((DEV,)), dma, dma],
        compiler_params=pltpu.CompilerParams(collective_id=2, has_side_effects=True,
                                             vmem_limit_bytes=63 * 1024 * 1024),
        name="fine",
    )(slots, req, ftab, gtab, src_pts, src_cluster.reshape(16, 128), tiles.reshape(DEV * 9, 8, 128), tgt_cluster.reshape(64, 128), incoming)


def on_device(src_cent, tgt_cent, src_mass, tgt_mass, src_pts, tgt_pts, src_cluster, tgt_cluster, support):
    req, slots = make_requests(support)
    ftab, gtab, tiles, incoming = coarse(src_cent, src_mass, tgt_cent, tgt_mass, req, tgt_pts, tgt_cluster)
    cf, cg, ff, fg = fine(slots, req, ftab, gtab, src_pts, src_cluster, tiles, tgt_cluster, incoming)
    return cf.reshape(-1), cg.reshape(-1), ff.reshape(-1), fg.reshape(-1)


def solution(mesh):
    both = ("row", "col")
    in_specs = (P(None, "row"), P(None, "col"), P("row"), P("col"), P(None, both), P(None, both), P(both), P(both),
                P(both, None))
    out_specs = (P("row"), P("col"), P(both), P(both))
    return jax.shard_map(on_device, mesh=mesh, in_specs=in_specs, out_specs=out_specs, check_vma=False)
```

```python
import math

import jax
import jax.numpy as jnp
from jax import lax
from jax.experimental import pallas as pl
from jax.experimental.pallas import tpu as pltpu
from jax.sharding import PartitionSpec as P

MESH = pl.DeviceIdType.MESH
F = 16
BLK = 256
SUPP = 16
SB_DEV = 8
TB_DEV = 32
KS = 4096
KT = 4096
EPS = 0.1
KAPPA = math.log2(math.e) / EPS
UNIT = EPS * math.log(2.0)
DEV = 128
STRIDE = 37
UNR = 4
PART = KS // 4
CH = 64
NJ = KT // 128
VMEM = pl.BlockSpec(memory_space=pltpu.VMEM)
SMEM = pl.BlockSpec(memory_space=pltpu.SMEM)
f32 = jnp.float32
i32 = jnp.int32
bf16 = jnp.bfloat16


def split3(v):
    hi = v.astype(bf16)
    rest = v - hi.astype(f32)
    mid = rest.astype(bf16)
    return hi, mid, (rest - mid.astype(f32)).astype(bf16)


def stack(pts, term, left):
    h, m, l = split3(pts)
    n = pts.shape[1]
    th, tm, tl = [v.astype(f32) for v in split3(term)]
    rid = lax.broadcasted_iota(i32, (16, n), 0)
    base, ones = (0, 3) if left else (3, 0)
    extra = jnp.where(rid == base, th, jnp.where(rid == base + 1, tm, jnp.where(rid == base + 2, tl, 0.0)))
    extra = jnp.where((rid >= ones) & (rid < ones + 3), 1.0, extra).astype(bf16)
    zero = jnp.zeros((16, n), bf16)
    if left:
        return jnp.concatenate([h, h, m, h, l, m, extra, zero], 0)
    return jnp.concatenate([h, m, h, l, h, m, extra, zero], 0)


def left_rows(x, dual=0.0):
    term = dual - KAPPA * jnp.sum(x * x, 0, keepdims=True)
    return stack((2.0 * KAPPA) * x, term, True).astype(f32).T.astype(bf16)


def spread(row):
    return jnp.broadcast_to(row, (128, 128)).T


def block(j, width=128):
    return slice(j * width, (j + 1) * width)


def place(index):
    return {"row": lax.div(index, 32), "col": lax.rem(index, 32)}


def remote(src, dst, ssem, rsem, where):
    return pltpu.make_async_remote_copy(src_ref=src, dst_ref=dst, send_sem=ssem, recv_sem=rsem, device_id=where,
                                        device_id_type=MESH)


def each(n, body):
    def step(i, c):
        body(i)
        return c

    lax.fori_loop(0, n, step, 0)


def lookup(tab, idx):
    low = idx & 127
    high = idx >> 7
    out = jnp.zeros((8, 128), f32)
    for r in range(32):
        got = jnp.take_along_axis(jnp.broadcast_to(tab[r:r + 1, :], (8, 128)), low, axis=1)
        out = jnp.where(high == r, got, out)
    return out


def request_kernel(sup_ref, req_ref, slot_ref):
    wanted = sup_ref[...].astype(f32)
    owner = jnp.floor(wanted * (1.0 / TB_DEV))
    local = wanted - owner * TB_DEV
    sub = lax.broadcasted_iota(i32, (128, 128), 0)
    lane = lax.broadcasted_iota(i32, (128, 128), 1)
    lanef = lane.astype(f32)
    same = jnp.broadcast_to(owner, (128, 128)) == sub.astype(f32)
    lo = jnp.min(jnp.where(same, lanef, 1e6), 1, keepdims=True)
    hi = jnp.max(jnp.where(same, lanef, -1.0), 1, keepdims=True)
    locb = jnp.broadcast_to(local, (128, 128)) + 1.0
    id0 = jnp.sum(jnp.where(lanef == lo, locb, 0.0), 1, keepdims=True) - 1.0
    id1 = jnp.sum(jnp.where((lanef == hi) & (hi > lo), locb, 0.0), 1, keepdims=True) - 1.0
    some = jnp.maximum(hi, 0.0)
    row = jnp.where(lane == 0, id0, jnp.where(lane == 1, id1, jnp.where(lane == 2, jnp.minimum(lo, some), jnp.where(
        lane == 3, some, jnp.where(lane == 4, jnp.maximum(id0, 0.0), jnp.maximum(id1, 0.0))))))
    req_ref[:, 0, :] = row.astype(i32)
    ownc = spread(owner)
    before = jnp.where((ownc == jnp.broadcast_to(owner, (128, 128))) & (sub < lane), 1.0, 0.0)
    second = jnp.sum(before, 0, keepdims=True)
    out = jnp.concatenate([owner, second, owner, owner], 0)
    slot_ref[...] = out.astype(i32)


def make_requests(support):
    return pl.pallas_call(
        request_kernel,
        out_shape=(jax.ShapeDtypeStruct((128, 1, 128), i32), jax.ShapeDtypeStruct((4, 128), i32)),
        in_specs=[VMEM], out_specs=(VMEM, VMEM), name="make_requests",
    )(support.reshape(1, 128))


def kernel(req_s, slot_ref, req_ref, src_in, smass_in, tgt_in, tmass_in, pts_ref, clu_ref, src_ref, sclu_ref, oclu_ref,
           out_ref,
           ftab_ref, gtab_ref, tiles_ref, inc_ref,
           src_all, smass_all, tgt_all, tmass_all, inc_s, blocks, out_buf,
                  a_scr, t0, t1, ys, xs, gp, lb, acc, fst, am, sh, mxs, rs, rbuf, fbuf,
                  send_sem, recv_sem, cs_sem, cr_sem, qs_sem, qr_sem, bs_sem, br_sem, lsem,
           gs, fs, sg, ccl, xt0, xt1, cm, sc0, sc1, rm0, rm1, sa, lse, back, ret, idr, mt, ex, ssem, rsem):
    row = lax.axis_index("row")
    col = lax.axis_index("col")
    me = row * 32 + col
    core = lax.rem(col, 2)
    quarter = lax.rem(row, 2) * 2 + core
    barrier = pltpu.get_barrier_semaphore()
    each(DEV - 1, lambda d: pl.semaphore_signal(barrier, inc=1, device_id=place(lax.rem(me + d + 1, DEV)),
                                                device_id_type=MESH))

    def quarter_of(r):
        return pl.ds(pl.multiple_of((lax.rem(r, 2) * 2 + core) * 256, 256), 256)


    def tgt_copy(d, a):
        where = {"row": row, "col": lax.rem(col + d + 1, 32)}
        src, dst = ((tgt_in, tgt_all), (tmass_in, tmass_all))[a]
        return remote(src, dst.at[col], cs_sem.at[d, a], cr_sem.at[d, a], where)

    def src_copy(d, a):
        to = lax.rem(row + d + 1, 4)
        src, dst = ((src_in, src_all), (smass_in, smass_all))[a]
        return remote(src.at[:, quarter_of(to)], dst.at[row], cs_sem.at[31 + d, a], cr_sem.at[31 + d, a],
                      {"row": to, "col": col})

    def req_copy(d):
        to = lax.rem(me + d + 1, DEV)
        return remote(req_ref.at[to], inc_ref.at[me], qs_sem.at[d], qr_sem.at[d], place(to))

    def blk_copy(d):
        to = lax.rem(me + lax.rem((d + 1) * STRIDE, DEV), DEV)
        return remote(out_buf.at[to], tiles_ref.at[me], bs_sem.at[d], br_sem.at[d], place(to))

    for t in range(TB_DEV):
        for h in range(2):
            blocks[t, h * 16:h * 16 + 16, :] = pts_ref[:, block(2 * t + h)]
    local = [pltpu.make_async_copy(tgt_in, tgt_all.at[col], lsem.at[0]),
             pltpu.make_async_copy(tmass_in, tmass_all.at[col], lsem.at[1]),
             pltpu.make_async_copy(src_in.at[:, quarter_of(row)], src_all.at[row], lsem.at[2]),
             pltpu.make_async_copy(smass_in.at[:, quarter_of(row)], smass_all.at[row], lsem.at[3]),
             pltpu.make_async_copy(req_ref.at[me], inc_ref.at[me], lsem.at[4])]
    for c in local:
        c.start()
    pl.semaphore_wait(barrier, DEV - 1)

    def start_src(d):
        src_copy(d, 0).start()
        src_copy(d, 1).start()

    def start_tgt(d):
        tgt_copy(d, 0).start()
        tgt_copy(d, 1).start()

    def wait_src(d):
        src_copy(d, 0).wait()
        src_copy(d, 1).wait()

    def wait_tgt(d):
        tgt_copy(d, 0).wait()
        tgt_copy(d, 1).wait()

    each(DEV - 1, lambda d: req_copy(d).start())
    each(3, start_src)
    each(31, start_tgt)
    for c in local:
        c.wait()
    each(3, wait_src)
    each(31, wait_tgt)
    for k in range(32):
        y = tgt_all[k]
        lbk = jnp.log2(tmass_all[k])
        ys[:, block(k)] = stack(y, lbk - KAPPA * jnp.sum(y * y, 0, keepdims=True), False)
        lb[:, block(k)] = jnp.broadcast_to(lbk, (8, 128))
    for q in range(4):
        for h in range(2):
            r0 = q * 256 + h * 128
            xs[r0:r0 + 128, :] = left_rows(src_all[q, :, block(h)])
            am[r0:r0 + 128, :] = spread(smass_all[q, :, block(h)])

    each(DEV - 1, lambda d: req_copy(d).wait())
    to_scalar = pltpu.make_async_copy(inc_ref, inc_s, lsem.at[5])
    to_scalar.start()
    to_scalar.wait()

    def fill(p):
        for q in range(2):
            t = inc_s[p, 0, 4 + q]
            out_buf[p, q * 32:q * 32 + 32, :] = blocks[t]
            out_buf[p, 64 + 2 * q:66 + 2 * q, :] = clu_ref[t].astype(f32)
        out_buf[p, 68:72, :] = jnp.zeros((4, 128), f32)

    each(DEV, fill)
    each(43, lambda d: blk_copy(d).start())
    own_block = pltpu.make_async_copy(out_buf.at[me], tiles_ref.at[me], lsem.at[6])
    own_block.start()

    acc[...] = jnp.full_like(acc, -jnp.inf)

    def rows_of(n):
        return pl.ds(pl.multiple_of(n * CH, CH), CH)

    def first(b):
        wide = pl.ds(pl.multiple_of(b * 256, 256), 256)
        mx = jnp.full((256, 128), -jnp.inf, f32)
        for c in range(NJ // 2):
            d = jnp.dot(xs[wide, :], ys[:, block(c, 256)], preferred_element_type=f32)
            a_scr[wide, block(c, 256)] = d
            mx = jnp.maximum(mx, jnp.maximum(d[:, :128], d[:, 128:]))
        mxs[...] = jnp.broadcast_to(jnp.max(mx, 1, keepdims=True), (256, 128))
        fl = None
        for q in range(5):
            now, prev = rows_of(4 * b + q), rows_of(4 * b + q - 1)
            s = None
            for j in range(NJ):
                if q < 4:
                    e = jnp.exp2(a_scr[now, block(j)] - mxs[block(q, CH), :])
                    s = e if s is None else s + e
                if q > 0:
                    v = a_scr[prev, block(j)] + fl
                    acc[:, block(j)] = jnp.maximum(acc[:, block(j)], jnp.max(v.reshape(CH // 8, 8, 128), 0))
            if q < 4:
                f1 = -(mxs[block(q, CH), :] + jnp.log2(jnp.broadcast_to(jnp.sum(s, 1, keepdims=True), (CH, 128))))
                fst[now, :] = f1
                fl = f1 + jnp.log2(am[now, :])

    each(PART // 256, first)
    for j in range(NJ):
        gp[:, block(j)] = jnp.broadcast_to(jnp.max(acc[:, block(j)], 0, keepdims=True), (8, 128))
    acc[...] = jnp.zeros_like(acc)

    def second(c):
        fl = fst[rows_of(c), :] + jnp.log2(am[rows_of(c), :])
        for j in range(NJ):
            v = a_scr[rows_of(c), block(j)] + fl
            a_scr[rows_of(c), block(j)] = v
            v = jnp.exp2(v.reshape(CH // 8, 8, 128) - gp[:, block(j)][None])
            acc[:, block(j)] = acc[:, block(j)] + jnp.sum(v, 0)

    each(PART // CH, second)
    for j in range(NJ):
        rbuf[0, quarter, :, block(j)] = gp[:1, block(j)] + jnp.log2(jnp.sum(acc[:, block(j)], 0, keepdims=True))

    def to_group(buf, k):
        out = []
        for d in range(3):
            to = lax.rem(quarter + d + 1, 4)
            where = {"row": row - lax.rem(row, 2) + lax.div(to, 2), "col": col - core + lax.rem(to, 2)}
            out.append(remote(buf, buf, send_sem.at[k, d], recv_sem.at[k, d], where))
        return out

    def swap(k, send=True):
        copies = to_group(rbuf.at[k, quarter], k)
        for c in copies:
            c.start()
        if send:
            each(12, lambda d: blk_copy(43 + 12 * k + d).start())
        for c in copies:
            c.wait()

    swap(0)
    for j in range(NJ):
        ls = [rbuf[0, i, :, block(j)] for i in range(4)]
        m = jnp.maximum(jnp.maximum(ls[0], ls[1]), jnp.maximum(ls[2], ls[3]))
        l = m + jnp.log2(sum(jnp.exp2(v - m) for v in ls))
        gp[:, block(j)] = lb[:, block(j)] - jnp.broadcast_to(l, (8, 128))

    def turn(k, renew=False, send=True):
        acc[...] = jnp.zeros_like(acc)

        def both(tn, n, tp, p):
            if tp is not None:
                rows = rows_of(p)
                u = am[rows, :] / jnp.broadcast_to(jnp.sum(rs[...], 1, keepdims=True), (CH, 128))
                sh[rows, :] = -jnp.log2(u)
            if tn is not None:
                rows = rows_of(n)
                if renew:
                    move = sh[rows, :]
                    fst[rows, :] = fst[rows, :] - move
            r = None
            for j in range(NJ):
                if tn is not None:
                    v = a_scr[rows, block(j)]
                    if renew:
                        v = v - move
                        a_scr[rows, block(j)] = v
                    e = jnp.exp2(v.reshape(CH // 8, 8, 128) + gp[:, block(j)][None]).reshape(CH, 128)
                    tn[:, block(j)] = e
                    r = e if r is None else r + e
                if tp is not None:
                    v = (tp[:, block(j)] * u).reshape(CH // 8, 8, 128)
                    acc[:, block(j)] = acc[:, block(j)] + jnp.sum(v, 0)
            if tn is not None:
                rs[...] = r

        def chunk(c):
            both(t1, 2 * c + 1, t0, 2 * c)
            both(t0, 2 * c + 2, t1, 2 * c + 1)

        last = PART // CH - 1
        both(t0, 0, None, None)
        each(last // 2, chunk)
        both(t1, last, t0, last - 1)
        both(None, None, t1, last)
        for j in range(NJ):
            rbuf[k, quarter, :, block(j)] = jnp.sum(acc[:, block(j)], 0, keepdims=True)
        swap(k, send)
        for j in range(NJ):
            c = jnp.broadcast_to(sum(rbuf[k, i, :, block(j)] for i in range(4)), (8, 128))
            gp[:, block(j)] = gp[:, block(j)] + (lb[:, block(j)] - jnp.log2(c))

    each(3, lambda i: turn(i + 1))
    turn(4, renew=True)
    each(2, lambda i: turn(i + 5))
    turn(7, send=False)
    for h in range(8):
        fbuf[quarter, h:h + 1, :] = ((fst[block(h), :] - sh[block(h), :]) * UNIT).T[:1, :]
    copies = to_group(fbuf.at[quarter], 8)
    for c in copies:
        c.start()
    for j in range(NJ):
        gtab_ref[j:j + 1, :] = gp[:1, block(j)] * UNIT
    for c in copies:
        c.wait()
    for q in range(4):
        for i in range(4):
            ftab_ref[q * 8 + 2 * i:q * 8 + 2 * i + 2, :] = fbuf[i, 2 * q:2 * q + 2, :]
    out_ref[0:8, :] = ftab_ref[pl.ds(pl.multiple_of(row * 8, 8), 8), :]
    out_ref[8:9, :] = gtab_ref[pl.ds(col, 1), :]
    ft = ftab_ref[...] * KAPPA
    gt = gtab_ref[...] * KAPPA

    def clusters(e):
        pair = tiles_ref[slot_ref[2, e]]
        second = slot_ref[1, e].astype(f32) > 0.5
        ccl[pl.ds(2 * e, 2), :] = jnp.where(second, pair[66:68], pair[64:66])

    for r in range(2):
        fs[block(r, 8), :] = lookup(ft, sclu_ref[block(r, 8), :])

    def own(r):
        rows = pl.ds(pl.multiple_of(r * 8, 8), 8)
        sg[rows, :] = lookup(gt, oclu_ref[rows, :])

    each(8, own)
    own_block.wait()
    each(DEV - 1, lambda d: blk_copy(d).wait())
    each(DEV, clusters)

    def sent(r):
        rows = pl.ds(pl.multiple_of(r * 8, 8), 8)
        gs[rows, :] = lookup(gt, ccl[rows, :].astype(i32))

    each(32, sent)

    def left(b, xt):
        for h in range(2):
            x = src_ref[:, pl.ds(pl.multiple_of(b * BLK + h * 128, 128), 128)]
            xt[block(h), :] = left_rows(x, fs[pl.ds(2 * b + h, 1), :])

    def duals(e):
        return [gs[pl.ds(2 * e + h, 1), :] for h in range(2)]

    def pair_product(b, k, xt, sc, rm, cm):
        e = b * SUPP + k
        i = slot_ref[2, e]
        second = slot_ref[1, e].astype(f32) > 0.5
        y = jnp.where(second, tiles_ref[i, 32:64, :], tiles_ref[i, 0:32, :])
        y = jnp.concatenate([y[:16], y[16:]], 1)
        st = stack(y, jnp.concatenate(duals(e), 1) - KAPPA * jnp.sum(y * y, 0, keepdims=True), False)
        d = jnp.dot(xt[...], st, preferred_element_type=f32)
        sc[k] = d
        rm[...] = jnp.maximum(rm[...], jnp.maximum(d[:, :128], d[:, 128:]))
        cm[k] = jnp.broadcast_to(jnp.max(d, 0, keepdims=True), (8, BLK))

    def col_part(b, k, sc, cm):
        g = duals(b * SUPP + k)
        for h in range(2):
            m = cm[k, :, block(h)]
            s = jnp.sum(jnp.exp2(sc[k, :, block(h)].reshape(BLK // 8, 8, 128) - m[None]), 0)
            lse[b * SUPP + k, h:h + 1, :] = m[:1] + jnp.log2(jnp.sum(s, 0, keepdims=True)) - g[h]

    def row_part(ks, sc, rm):
        for r in range(BLK // 64):
            m = rm[block(r, 64), :]
            s = sa[block(r, 64), :]
            for k in ks:
                s = s + (jnp.exp2(sc[k, block(r, 64), :128] - m) + jnp.exp2(sc[k, block(r, 64), 128:] - m))
            sa[block(r, 64), :] = s

    def one(b, xt, sc, rm, prev):
        left(b, xt)
        rm[...] = jnp.full_like(rm, -jnp.inf)
        for u in range(UNR):
            pair_product(b, u, xt, sc, rm, cm)
        if prev is not None:
            sa[...] = jnp.zeros_like(sa)

        def some(g):
            for u in range(UNR):
                col_part(b, UNR * g + u, sc, cm)
            if prev is not None:
                row_part([UNR * g + u for u in range(UNR)], *prev)
            for u in range(UNR):
                pair_product(b, lax.rem(UNR * g + UNR + u, SUPP), xt, sc, rm, cm)

        each(SUPP // UNR, some)
        rm[...] = jnp.broadcast_to(jnp.max(rm[...], 1, keepdims=True), (BLK, 128))
        if prev is not None:
            finish(b - 1, prev[1])

    def finish(b, rm):
        out = rm[...] + jnp.log2(jnp.sum(sa[...], 1, keepdims=True)) - math.log2(SUPP * BLK)
        for h in range(2):
            mine = fs[pl.ds(2 * b + h, 1), :]
            out_ref[pl.ds(16 + 2 * b + h, 1), :] = (0.5 * UNIT) * (mine - (out[block(h), :].T[:1, :] - mine))

    one(0, xt0, sc0, rm0, None)

    def two(p):
        one(2 * p + 1, xt1, sc1, rm1, (sc0, rm0))
        one(2 * p + 2, xt0, sc0, rm0, (sc1, rm1))

    each(3, two)
    one(7, xt1, sc1, rm1, (sc0, rm0))

    def fill_back(p):
        for q in range(2):
            back[p, 2 * q:2 * q + 2, :] = lse[req_s[p, 0, 2 + q]]

    each(DEV, fill_back)

    def ret_copy(d):
        to = lax.rem(me + d + 1, DEV)
        return remote(back.at[to], ret.at[me], ssem.at[d], rsem.at[d], place(to))

    each(DEV - 1, lambda d: ret_copy(d).start())
    mine = pltpu.make_async_copy(back.at[me], ret.at[me], lsem.at[8])
    mine.start()
    sa[...] = jnp.zeros_like(sa)

    each(SUPP // 2, lambda g: row_part((2 * g, 2 * g + 1), sc1, rm1))
    finish(7, rm1)
    lane = lax.broadcasted_iota(i32, (DEV, 128), 1).astype(f32)
    sub = lax.broadcasted_iota(i32, (DEV, 128), 0).astype(f32)
    hot, hot_t = [], []
    for q in range(2):
        idv = jnp.broadcast_to(inc_ref[:, 0, q:q + 1].astype(f32), (DEV, 128))
        idr[q] = idv
        hot.append(jnp.where(idv == lane, 1.0, 0.0).astype(bf16))
        hot_t.append(jnp.where(idv.T == sub, 1.0, 0.0).astype(bf16))
    count = sum(jnp.sum(h.astype(f32), 1, keepdims=True) for h in hot_t)
    mt[...] = jnp.zeros_like(mt)
    mine.wait()
    each(DEV - 1, lambda d: ret_copy(d).wait())
    for q in range(2):
        for h in range(2):
            ex[q, h] = ret[:, 2 * q + h, :]

    def tops(t):
        tf = t.astype(f32)
        for h in range(2):
            m = jnp.maximum(jnp.where(idr[0] == tf, ex[0, h], -jnp.inf), jnp.where(idr[1] == tf, ex[1, h], -jnp.inf))
            mt[h, pl.ds(t, 1), :] = jnp.max(m, 0, keepdims=True)

    each(TB_DEV, tops)
    for h in range(2):
        tot = jnp.zeros((DEV, 128), f32)
        mparts = split3(mt[h])
        for q in range(2):
            mx = sum(jnp.dot(hot[q], mp, preferred_element_type=f32) for mp in mparts)
            e = jnp.where(idr[q] >= 0.0, jnp.exp2(ex[q, h] - mx), 0.0)
            tot = tot + sum(jnp.dot(hot_t[q], ep, preferred_element_type=f32) for ep in split3(e))
        ex[0, h] = mt[h] + jnp.log2(tot) - jnp.log2(jnp.broadcast_to(count, (DEV, 128)) * BLK)
    for t in range(TB_DEV):
        for h in range(2):
            out_ref[32 + 2 * t + h:33 + 2 * t + h, :] = (0.5 * UNIT) * (sg[2 * t + h:2 * t + h + 1, :] - ex[0, h, t:t + 1, :])


def split_kernel(all_ref, cf_ref, cg_ref, ff_ref, fg_ref):
    cf_ref[...] = all_ref[0:8, :]
    cg_ref[...] = all_ref[8:9, :]
    ff_ref[...] = all_ref[16:32, :]
    fg_ref[...] = all_ref[32:96, :]


def on_device(src_cent, tgt_cent, src_mass, tgt_mass, src_pts, tgt_pts, src_cluster, tgt_cluster, support):
    V = pltpu.VMEM
    S = jax.ShapeDtypeStruct
    dma = pltpu.SemaphoreType.DMA
    req, slots = make_requests(support)
    out = pl.pallas_call(
        kernel,
        out_shape=S((96, 128), f32),
        in_specs=[SMEM] * 2 + [VMEM] * 10,
        out_specs=VMEM,
        scratch_shapes=[V((32, 128), f32), V((32, 128), f32), V((DEV, 72, 128), f32),
                        V((DEV, 1, 128), i32),
                        V((4, F, 256), f32), V((4, 1, 256), f32), V((32, F, 128), f32), V((32, 1, 128), f32),
                        pltpu.SMEM((DEV, 1, 128), i32), V((TB_DEV, 32, 128), f32), V((DEV, 72, 128), f32),
                        V((PART, KT), f32), V((CH, KT), f32), V((CH, KT), f32),
                        V((128, KT), bf16), V((PART, 128), bf16), V((8, KT), f32), V((8, KT), f32), V((8, KT), f32),
                        V((PART, 128), f32), V((PART, 128), f32), V((PART, 128), f32), V((256, 128), f32),
                        V((CH, 128), f32), V((8, 4, 1, KT), f32), V((4, 8, 128), f32),
                        dma((9, 3)), dma((9, 3)), dma((34, 2)), dma((34, 2)),
                        dma((DEV,)), dma((DEV,)), dma((DEV,)), dma((DEV,)), dma((9,)),
                        V((2 * DEV, 128), f32), V((16, 128), f32), V((64, 128), f32), V((2 * DEV, 128), f32),
                        V((BLK, 128), bf16), V((BLK, 128), bf16), V((SUPP, 8, BLK), f32),
                        V((SUPP, BLK, BLK), f32), V((SUPP, BLK, BLK), f32), V((BLK, 128), f32), V((BLK, 128), f32),
                        V((BLK, 128), f32), V((DEV, 2, 128), f32), V((DEV, 4, 128), f32), V((DEV, 4, 128), f32),
                        V((2, DEV, 128), f32), V((2, DEV, 128), f32), V((2, 2, DEV, 128), f32),
                        dma((DEV,)), dma((DEV,))],
        compiler_params=pltpu.CompilerParams(collective_id=1, has_side_effects=True,
                                             vmem_limit_bytes=63 * 1024 * 1024),
        name="transport",
    )(req, slots, req, src_cent, src_mass.reshape(1, -1), tgt_cent, tgt_mass.reshape(1, -1), tgt_pts,
      tgt_cluster.reshape(TB_DEV, 2, 128), src_pts, src_cluster.reshape(16, 128), tgt_cluster.reshape(64, 128))
    cf, cg, ff, fg = pl.pallas_call(
        split_kernel,
        out_shape=(S((8, 128), f32), S((1, 128), f32), S((16, 128), f32), S((64, 128), f32)),
        in_specs=[VMEM], out_specs=(VMEM,) * 4, name="split",
    )(out)
    return cf.reshape(-1), cg.reshape(-1), ff.reshape(-1), fg.reshape(-1)


def solution(mesh):
    both = ("row", "col")
    in_specs = (P(None, "row"), P(None, "col"), P("row"), P("col"), P(None, both), P(None, both), P(both), P(both),
                P(both, None))
    out_specs = (P("row"), P("col"), P(both), P(both))
    return jax.shard_map(on_device, mesh=mesh, in_specs=in_specs, out_specs=out_specs, check_vma=False)
```

```python
import math

import jax
import jax.numpy as jnp
from jax import lax
from jax.experimental import pallas as pl
from jax.experimental.pallas import tpu as pltpu
from jax.sharding import PartitionSpec as P

MESH = pl.DeviceIdType.MESH
F = 16
BLK = 256
SUPP = 16
SB_DEV = 8
TB_DEV = 32
KS = 4096
KT = 4096
EPS = 0.1
KAPPA = math.log2(math.e) / EPS
UNIT = EPS * math.log(2.0)
DEV = 128
STRIDE = 37
UNR = 4
PART = KS // 4
CH = 64
NJ = KT // 128
VMEM = pl.BlockSpec(memory_space=pltpu.VMEM)
SMEM = pl.BlockSpec(memory_space=pltpu.SMEM)
f32 = jnp.float32
i32 = jnp.int32
bf16 = jnp.bfloat16


def split3(v):
    hi = v.astype(bf16)
    rest = v - hi.astype(f32)
    mid = rest.astype(bf16)
    return hi, mid, (rest - mid.astype(f32)).astype(bf16)


def stack(pts, term, left):
    h, m, l = split3(pts)
    n = pts.shape[1]
    th, tm, tl = [v.astype(f32) for v in split3(term)]
    rid = lax.broadcasted_iota(i32, (16, n), 0)
    base, ones = (0, 3) if left else (3, 0)
    extra = jnp.where(rid == base, th, jnp.where(rid == base + 1, tm, jnp.where(rid == base + 2, tl, 0.0)))
    extra = jnp.where((rid >= ones) & (rid < ones + 3), 1.0, extra).astype(bf16)
    zero = jnp.zeros((16, n), bf16)
    if left:
        return jnp.concatenate([h, h, m, h, l, m, extra, zero], 0)
    return jnp.concatenate([h, m, h, l, h, m, extra, zero], 0)


def left_rows(x, dual=0.0):
    term = dual - KAPPA * jnp.sum(x * x, 0, keepdims=True)
    return stack((2.0 * KAPPA) * x, term, True).astype(f32).T.astype(bf16)


def spread(row):
    return jnp.broadcast_to(row, (128, 128)).T


def block(j, width=128):
    return slice(j * width, (j + 1) * width)


def place(index):
    return {"row": lax.div(index, 32), "col": lax.rem(index, 32)}


def remote(src, dst, ssem, rsem, where):
    return pltpu.make_async_remote_copy(src_ref=src, dst_ref=dst, send_sem=ssem, recv_sem=rsem, device_id=where,
                                        device_id_type=MESH)


def each(n, body):
    def step(i, c):
        body(i)
        return c

    lax.fori_loop(0, n, step, 0)


def lookup(tab, idx):
    low = idx & 127
    high = idx >> 7
    out = jnp.zeros((8, 128), f32)
    for r in range(32):
        got = jnp.take_along_axis(jnp.broadcast_to(tab[r:r + 1, :], (8, 128)), low, axis=1)
        out = jnp.where(high == r, got, out)
    return out


def request_kernel(sup_ref, req_ref, slot_ref):
    wanted = sup_ref[...].astype(f32)
    owner = jnp.floor(wanted * (1.0 / TB_DEV))
    local = wanted - owner * TB_DEV
    sub = lax.broadcasted_iota(i32, (128, 128), 0)
    lane = lax.broadcasted_iota(i32, (128, 128), 1)
    lanef = lane.astype(f32)
    same = jnp.broadcast_to(owner, (128, 128)) == sub.astype(f32)
    lo = jnp.min(jnp.where(same, lanef, 1e6), 1, keepdims=True)
    hi = jnp.max(jnp.where(same, lanef, -1.0), 1, keepdims=True)
    locb = jnp.broadcast_to(local, (128, 128)) + 1.0
    id0 = jnp.sum(jnp.where(lanef == lo, locb, 0.0), 1, keepdims=True) - 1.0
    id1 = jnp.sum(jnp.where((lanef == hi) & (hi > lo), locb, 0.0), 1, keepdims=True) - 1.0
    some = jnp.maximum(hi, 0.0)
    row = jnp.where(lane == 0, id0, jnp.where(lane == 1, id1, jnp.where(lane == 2, jnp.minimum(lo, some), jnp.where(
        lane == 3, some, jnp.where(lane == 4, jnp.maximum(id0, 0.0), jnp.maximum(id1, 0.0))))))
    req_ref[:, 0, :] = row.astype(i32)
    ownc = spread(owner)
    before = jnp.where((ownc == jnp.broadcast_to(owner, (128, 128))) & (sub < lane), 1.0, 0.0)
    second = jnp.sum(before, 0, keepdims=True)
    out = jnp.concatenate([owner, second, owner, owner], 0)
    slot_ref[...] = out.astype(i32)


def make_requests(support):
    return pl.pallas_call(
        request_kernel,
        out_shape=(jax.ShapeDtypeStruct((128, 1, 128), i32), jax.ShapeDtypeStruct((4, 128), i32)),
        in_specs=[VMEM], out_specs=(VMEM, VMEM), name="make_requests",
    )(support.reshape(1, 128))


def kernel(req_s, slot_ref, req_ref, src_in, smass_in, tgt_in, tmass_in, pts_ref, clu_ref, src_ref, sclu_ref, oclu_ref,
           out_ref,
           ftab_ref, gtab_ref, tiles_ref, inc_ref,
           src_all, smass_all, tgt_all, tmass_all, inc_s, blocks, out_buf,
                  a_scr, t0, t1, ys, xs, gp, lb, acc, fst, am, sh, mxs, rs, rbuf, fbuf,
                  send_sem, recv_sem, cs_sem, cr_sem, qs_sem, qr_sem, bs_sem, br_sem, lsem,
           gs, fs, sg, ccl, xt0, xt1, cm, sc0, sc1, rm0, rm1, sa, lse, back, ret, idr, mt, ex, ssem, rsem):
    row = lax.axis_index("row")
    col = lax.axis_index("col")
    me = row * 32 + col
    core = lax.rem(col, 2)
    quarter = lax.rem(row, 2) * 2 + core
    barrier = pltpu.get_barrier_semaphore()
    each(DEV - 1, lambda d: pl.semaphore_signal(barrier, inc=1, device_id=place(lax.rem(me + d + 1, DEV)),
                                                device_id_type=MESH))

    def quarter_of(r):
        return pl.ds(pl.multiple_of((lax.rem(r, 2) * 2 + core) * 256, 256), 256)


    def tgt_copy(d, a):
        where = {"row": row, "col": lax.rem(col + d + 1, 32)}
        src, dst = ((tgt_in, tgt_all), (tmass_in, tmass_all))[a]
        return remote(src, dst.at[col], cs_sem.at[d, a], cr_sem.at[d, a], where)

    def src_copy(d, a):
        to = lax.rem(row + d + 1, 4)
        src, dst = ((src_in, src_all), (smass_in, smass_all))[a]
        return remote(src.at[:, quarter_of(to)], dst.at[row], cs_sem.at[31 + d, a], cr_sem.at[31 + d, a],
                      {"row": to, "col": col})

    def req_copy(d):
        to = lax.rem(me + d + 1, DEV)
        return remote(req_ref.at[to], inc_ref.at[me], qs_sem.at[d], qr_sem.at[d], place(to))

    def blk_copy(d):
        to = lax.rem(me + lax.rem((d + 1) * STRIDE, DEV), DEV)
        return remote(out_buf.at[to], tiles_ref.at[me], bs_sem.at[d], br_sem.at[d], place(to))

    for t in range(TB_DEV):
        for h in range(2):
            blocks[t, h * 16:h * 16 + 16, :] = pts_ref[:, block(2 * t + h)]
    local = [pltpu.make_async_copy(tgt_in, tgt_all.at[col], lsem.at[0]),
             pltpu.make_async_copy(tmass_in, tmass_all.at[col], lsem.at[1]),
             pltpu.make_async_copy(src_in.at[:, quarter_of(row)], src_all.at[row], lsem.at[2]),
             pltpu.make_async_copy(smass_in.at[:, quarter_of(row)], smass_all.at[row], lsem.at[3]),
             pltpu.make_async_copy(req_ref.at[me], inc_ref.at[me], lsem.at[4])]
    for c in local:
        c.start()
    pl.semaphore_wait(barrier, DEV - 1)

    def start_src(d):
        src_copy(d, 0).start()
        src_copy(d, 1).start()

    def start_tgt(d):
        tgt_copy(d, 0).start()
        tgt_copy(d, 1).start()

    def wait_src(d):
        src_copy(d, 0).wait()
        src_copy(d, 1).wait()

    def wait_tgt(d):
        tgt_copy(d, 0).wait()
        tgt_copy(d, 1).wait()

    each(DEV - 1, lambda d: req_copy(d).start())
    each(3, start_src)
    each(31, start_tgt)
    for c in local:
        c.wait()
    each(3, wait_src)
    each(31, wait_tgt)
    for k in range(32):
        y = tgt_all[k]
        lbk = jnp.log2(tmass_all[k])
        ys[:, block(k)] = stack(y, lbk - KAPPA * jnp.sum(y * y, 0, keepdims=True), False)
        lb[:, block(k)] = jnp.broadcast_to(lbk, (8, 128))
    for q in range(4):
        for h in range(2):
            r0 = q * 256 + h * 128
            xs[r0:r0 + 128, :] = left_rows(src_all[q, :, block(h)])
            am[r0:r0 + 128, :] = spread(smass_all[q, :, block(h)])

    each(DEV - 1, lambda d: req_copy(d).wait())
    to_scalar = pltpu.make_async_copy(inc_ref, inc_s, lsem.at[5])
    to_scalar.start()
    to_scalar.wait()

    def fill(p):
        for q in range(2):
            t = inc_s[p, 0, 4 + q]
            out_buf[p, q * 32:q * 32 + 32, :] = blocks[t]
            out_buf[p, 64 + 2 * q:66 + 2 * q, :] = clu_ref[t].astype(f32)
        out_buf[p, 68:72, :] = jnp.zeros((4, 128), f32)

    each(DEV, fill)
    each(71, lambda d: blk_copy(d).start())
    own_block = pltpu.make_async_copy(out_buf.at[me], tiles_ref.at[me], lsem.at[6])
    own_block.start()

    acc[...] = jnp.full_like(acc, -jnp.inf)

    def rows_of(n):
        return pl.ds(pl.multiple_of(n * CH, CH), CH)

    def first(b):
        wide = pl.ds(pl.multiple_of(b * 256, 256), 256)
        mx = jnp.full((256, 128), -jnp.inf, f32)
        for c in range(NJ // 2):
            d = jnp.dot(xs[wide, :], ys[:, block(c, 256)], preferred_element_type=f32)
            a_scr[wide, block(c, 256)] = d
            mx = jnp.maximum(mx, jnp.maximum(d[:, :128], d[:, 128:]))
        mxs[...] = jnp.broadcast_to(jnp.max(mx, 1, keepdims=True), (256, 128))
        fl = None
        for q in range(5):
            now, prev = rows_of(4 * b + q), rows_of(4 * b + q - 1)
            s = None
            for j in range(NJ):
                if q < 4:
                    e = jnp.exp2(a_scr[now, block(j)] - mxs[block(q, CH), :])
                    s = e if s is None else s + e
                if q > 0:
                    v = a_scr[prev, block(j)] + fl
                    acc[:, block(j)] = jnp.maximum(acc[:, block(j)], jnp.max(v.reshape(CH // 8, 8, 128), 0))
            if q < 4:
                f1 = -(mxs[block(q, CH), :] + jnp.log2(jnp.broadcast_to(jnp.sum(s, 1, keepdims=True), (CH, 128))))
                fst[now, :] = f1
                fl = f1 + jnp.log2(am[now, :])

    each(PART // 256, first)
    for j in range(NJ):
        gp[:, block(j)] = jnp.broadcast_to(jnp.max(acc[:, block(j)], 0, keepdims=True), (8, 128))
    acc[...] = jnp.zeros_like(acc)

    def second(c):
        fl = fst[rows_of(c), :] + jnp.log2(am[rows_of(c), :])
        for j in range(NJ):
            v = a_scr[rows_of(c), block(j)] + fl
            a_scr[rows_of(c), block(j)] = v
            v = jnp.exp2(v.reshape(CH // 8, 8, 128) - gp[:, block(j)][None])
            acc[:, block(j)] = acc[:, block(j)] + jnp.sum(v, 0)

    each(PART // CH, second)
    for j in range(NJ):
        rbuf[0, quarter, :, block(j)] = gp[:1, block(j)] + jnp.log2(jnp.sum(acc[:, block(j)], 0, keepdims=True))

    def to_group(buf, k):
        out = []
        for d in range(3):
            to = lax.rem(quarter + d + 1, 4)
            where = {"row": row - lax.rem(row, 2) + lax.div(to, 2), "col": col - core + lax.rem(to, 2)}
            out.append(remote(buf, buf, send_sem.at[k, d], recv_sem.at[k, d], where))
        return out

    def swap(k, send=True):
        copies = to_group(rbuf.at[k, quarter], k)
        for c in copies:
            c.start()
        if send:
            each(8, lambda d: blk_copy(71 + 8 * k + d).start())
        for c in copies:
            c.wait()

    swap(0)
    for j in range(NJ):
        ls = [rbuf[0, i, :, block(j)] for i in range(4)]
        m = jnp.maximum(jnp.maximum(ls[0], ls[1]), jnp.maximum(ls[2], ls[3]))
        l = m + jnp.log2(sum(jnp.exp2(v - m) for v in ls))
        gp[:, block(j)] = lb[:, block(j)] - jnp.broadcast_to(l, (8, 128))

    def turn(k, renew=False, send=True):
        acc[...] = jnp.zeros_like(acc)

        def both(tn, n, tp, p):
            if tp is not None:
                rows = rows_of(p)
                u = am[rows, :] / jnp.broadcast_to(jnp.sum(rs[...], 1, keepdims=True), (CH, 128))
                sh[rows, :] = -jnp.log2(u)
            if tn is not None:
                rows = rows_of(n)
                if renew:
                    move = sh[rows, :]
                    fst[rows, :] = fst[rows, :] - move
            r = None
            for j in range(NJ):
                if tn is not None:
                    v = a_scr[rows, block(j)]
                    if renew:
                        v = v - move
                        a_scr[rows, block(j)] = v
                    e = jnp.exp2(v.reshape(CH // 8, 8, 128) + gp[:, block(j)][None]).reshape(CH, 128)
                    tn[:, block(j)] = e
                    r = e if r is None else r + e
                if tp is not None:
                    v = (tp[:, block(j)] * u).reshape(CH // 8, 8, 128)
                    acc[:, block(j)] = acc[:, block(j)] + jnp.sum(v, 0)
            if tn is not None:
                rs[...] = r

        def chunk(c):
            both(t1, 2 * c + 1, t0, 2 * c)
            both(t0, 2 * c + 2, t1, 2 * c + 1)

        last = PART // CH - 1
        both(t0, 0, None, None)
        each(last // 2, chunk)
        both(t1, last, t0, last - 1)
        both(None, None, t1, last)
        for j in range(NJ):
            rbuf[k, quarter, :, block(j)] = jnp.sum(acc[:, block(j)], 0, keepdims=True)
        swap(k, send)
        for j in range(NJ):
            c = jnp.broadcast_to(sum(rbuf[k, i, :, block(j)] for i in range(4)), (8, 128))
            gp[:, block(j)] = gp[:, block(j)] + (lb[:, block(j)] - jnp.log2(c))

    each(3, lambda i: turn(i + 1))
    turn(4, renew=True)
    each(2, lambda i: turn(i + 5))
    turn(7, send=False)
    for h in range(8):
        fbuf[quarter, h:h + 1, :] = ((fst[block(h), :] - sh[block(h), :]) * UNIT).T[:1, :]
    copies = to_group(fbuf.at[quarter], 8)
    for c in copies:
        c.start()
    for j in range(NJ):
        gtab_ref[j:j + 1, :] = gp[:1, block(j)] * UNIT
    for c in copies:
        c.wait()
    for q in range(4):
        for i in range(4):
            ftab_ref[q * 8 + 2 * i:q * 8 + 2 * i + 2, :] = fbuf[i, 2 * q:2 * q + 2, :]
    out_ref[0:8, :] = ftab_ref[pl.ds(pl.multiple_of(row * 8, 8), 8), :]
    out_ref[8:9, :] = gtab_ref[pl.ds(col, 1), :]
    ft = ftab_ref[...] * KAPPA
    gt = gtab_ref[...] * KAPPA

    def clusters(e):
        pair = tiles_ref[slot_ref[2, e]]
        second = slot_ref[1, e].astype(f32) > 0.5
        ccl[pl.ds(2 * e, 2), :] = jnp.where(second, pair[66:68], pair[64:66])

    for r in range(2):
        fs[block(r, 8), :] = lookup(ft, sclu_ref[block(r, 8), :])

    def own(r):
        rows = pl.ds(pl.multiple_of(r * 8, 8), 8)
        sg[rows, :] = lookup(gt, oclu_ref[rows, :])

    each(8, own)
    own_block.wait()
    each(DEV - 1, lambda d: blk_copy(d).wait())
    each(DEV, clusters)

    def sent(r):
        rows = pl.ds(pl.multiple_of(r * 8, 8), 8)
        gs[rows, :] = lookup(gt, ccl[rows, :].astype(i32))

    each(32, sent)

    def left(b, xt):
        for h in range(2):
            x = src_ref[:, pl.ds(pl.multiple_of(b * BLK + h * 128, 128), 128)]
            xt[block(h), :] = left_rows(x, fs[pl.ds(2 * b + h, 1), :])

    def duals(e):
        return [gs[pl.ds(2 * e + h, 1), :] for h in range(2)]

    def pair_product(b, k, xt, sc, rm, cm):
        e = b * SUPP + k
        i = slot_ref[2, e]
        second = slot_ref[1, e].astype(f32) > 0.5
        y = jnp.where(second, tiles_ref[i, 32:64, :], tiles_ref[i, 0:32, :])
        y = jnp.concatenate([y[:16], y[16:]], 1)
        st = stack(y, jnp.concatenate(duals(e), 1) - KAPPA * jnp.sum(y * y, 0, keepdims=True), False)
        d = jnp.dot(xt[...], st, preferred_element_type=f32)
        sc[k] = d
        rm[...] = jnp.maximum(rm[...], jnp.maximum(d[:, :128], d[:, 128:]))
        cm[k] = jnp.broadcast_to(jnp.max(d, 0, keepdims=True), (8, BLK))

    def col_part(b, k, sc, cm):
        g = duals(b * SUPP + k)
        for h in range(2):
            m = cm[k, :, block(h)]
            s = jnp.sum(jnp.exp2(sc[k, :, block(h)].reshape(BLK // 8, 8, 128) - m[None]), 0)
            lse[b * SUPP + k, h:h + 1, :] = m[:1] + jnp.log2(jnp.sum(s, 0, keepdims=True)) - g[h]

    def row_part(ks, sc, rm):
        for r in range(BLK // 64):
            m = rm[block(r, 64), :]
            s = sa[block(r, 64), :]
            for k in ks:
                s = s + (jnp.exp2(sc[k, block(r, 64), :128] - m) + jnp.exp2(sc[k, block(r, 64), 128:] - m))
            sa[block(r, 64), :] = s

    def one(b, xt, sc, rm, prev):
        left(b, xt)
        rm[...] = jnp.full_like(rm, -jnp.inf)
        for u in range(UNR):
            pair_product(b, u, xt, sc, rm, cm)
        if prev is not None:
            sa[...] = jnp.zeros_like(sa)

        def some(g):
            for u in range(UNR):
                col_part(b, UNR * g + u, sc, cm)
            if prev is not None:
                row_part([UNR * g + u for u in range(UNR)], *prev)
            for u in range(UNR):
                pair_product(b, lax.rem(UNR * g + UNR + u, SUPP), xt, sc, rm, cm)

        each(SUPP // UNR, some)
        rm[...] = jnp.broadcast_to(jnp.max(rm[...], 1, keepdims=True), (BLK, 128))
        if prev is not None:
            finish(b - 1, prev[1])

    def finish(b, rm):
        out = rm[...] + jnp.log2(jnp.sum(sa[...], 1, keepdims=True)) - math.log2(SUPP * BLK)
        for h in range(2):
            mine = fs[pl.ds(2 * b + h, 1), :]
            out_ref[pl.ds(16 + 2 * b + h, 1), :] = (0.5 * UNIT) * (mine - (out[block(h), :].T[:1, :] - mine))

    one(0, xt0, sc0, rm0, None)

    def two(p):
        one(2 * p + 1, xt1, sc1, rm1, (sc0, rm0))
        one(2 * p + 2, xt0, sc0, rm0, (sc1, rm1))

    each(3, two)
    one(7, xt1, sc1, rm1, (sc0, rm0))

    def fill_back(p):
        for q in range(2):
            back[p, 2 * q:2 * q + 2, :] = lse[req_s[p, 0, 2 + q]]

    each(DEV, fill_back)

    def ret_copy(d):
        to = lax.rem(me + d + 1, DEV)
        return remote(back.at[to], ret.at[me], ssem.at[d], rsem.at[d], place(to))

    each(DEV - 1, lambda d: ret_copy(d).start())
    mine = pltpu.make_async_copy(back.at[me], ret.at[me], lsem.at[8])
    mine.start()
    sa[...] = jnp.zeros_like(sa)

    each(SUPP // 2, lambda g: row_part((2 * g, 2 * g + 1), sc1, rm1))
    finish(7, rm1)
    lane = lax.broadcasted_iota(i32, (DEV, 128), 1).astype(f32)
    sub = lax.broadcasted_iota(i32, (DEV, 128), 0).astype(f32)
    hot, hot_t = [], []
    for q in range(2):
        idv = jnp.broadcast_to(inc_ref[:, 0, q:q + 1].astype(f32), (DEV, 128))
        idr[q] = idv
        hot.append(jnp.where(idv == lane, 1.0, 0.0).astype(bf16))
        hot_t.append(jnp.where(idv.T == sub, 1.0, 0.0).astype(bf16))
    count = sum(jnp.sum(h.astype(f32), 1, keepdims=True) for h in hot_t)
    mt[...] = jnp.zeros_like(mt)
    mine.wait()
    each(DEV - 1, lambda d: ret_copy(d).wait())
    for q in range(2):
        for h in range(2):
            ex[q, h] = ret[:, 2 * q + h, :]

    def tops(t):
        tf = t.astype(f32)
        for h in range(2):
            m = jnp.maximum(jnp.where(idr[0] == tf, ex[0, h], -jnp.inf), jnp.where(idr[1] == tf, ex[1, h], -jnp.inf))
            mt[h, pl.ds(t, 1), :] = jnp.max(m, 0, keepdims=True)

    each(TB_DEV, tops)
    for h in range(2):
        tot = jnp.zeros((DEV, 128), f32)
        mparts = split3(mt[h])
        for q in range(2):
            mx = sum(jnp.dot(hot[q], mp, preferred_element_type=f32) for mp in mparts)
            e = jnp.where(idr[q] >= 0.0, jnp.exp2(ex[q, h] - mx), 0.0)
            tot = tot + sum(jnp.dot(hot_t[q], ep, preferred_element_type=f32) for ep in split3(e))
        ex[0, h] = mt[h] + jnp.log2(tot) - jnp.log2(jnp.broadcast_to(count, (DEV, 128)) * BLK)
    for t in range(TB_DEV):
        for h in range(2):
            out_ref[32 + 2 * t + h:33 + 2 * t + h, :] = (0.5 * UNIT) * (sg[2 * t + h:2 * t + h + 1, :] - ex[0, h, t:t + 1, :])


def split_kernel(all_ref, cf_ref, cg_ref, ff_ref, fg_ref):
    cf_ref[...] = all_ref[0:8, :]
    cg_ref[...] = all_ref[8:9, :]
    ff_ref[...] = all_ref[16:32, :]
    fg_ref[...] = all_ref[32:96, :]


def on_device(src_cent, tgt_cent, src_mass, tgt_mass, src_pts, tgt_pts, src_cluster, tgt_cluster, support):
    V = pltpu.VMEM
    S = jax.ShapeDtypeStruct
    dma = pltpu.SemaphoreType.DMA
    req, slots = make_requests(support)
    out = pl.pallas_call(
        kernel,
        out_shape=S((96, 128), f32),
        in_specs=[SMEM] * 2 + [VMEM] * 10,
        out_specs=VMEM,
        scratch_shapes=[V((32, 128), f32), V((32, 128), f32), V((DEV, 72, 128), f32),
                        V((DEV, 1, 128), i32),
                        V((4, F, 256), f32), V((4, 1, 256), f32), V((32, F, 128), f32), V((32, 1, 128), f32),
                        pltpu.SMEM((DEV, 1, 128), i32), V((TB_DEV, 32, 128), f32), V((DEV, 72, 128), f32),
                        V((PART, KT), f32), V((CH, KT), f32), V((CH, KT), f32),
                        V((128, KT), bf16), V((PART, 128), bf16), V((8, KT), f32), V((8, KT), f32), V((8, KT), f32),
                        V((PART, 128), f32), V((PART, 128), f32), V((PART, 128), f32), V((256, 128), f32),
                        V((CH, 128), f32), V((8, 4, 1, KT), f32), V((4, 8, 128), f32),
                        dma((9, 3)), dma((9, 3)), dma((34, 2)), dma((34, 2)),
                        dma((DEV,)), dma((DEV,)), dma((DEV,)), dma((DEV,)), dma((9,)),
                        V((2 * DEV, 128), f32), V((16, 128), f32), V((64, 128), f32), V((2 * DEV, 128), f32),
                        V((BLK, 128), bf16), V((BLK, 128), bf16), V((SUPP, 8, BLK), f32),
                        V((SUPP, BLK, BLK), f32), V((SUPP, BLK, BLK), f32), V((BLK, 128), f32), V((BLK, 128), f32),
                        V((BLK, 128), f32), V((DEV, 2, 128), f32), V((DEV, 4, 128), f32), V((DEV, 4, 128), f32),
                        V((2, DEV, 128), f32), V((2, DEV, 128), f32), V((2, 2, DEV, 128), f32),
                        dma((DEV,)), dma((DEV,))],
        compiler_params=pltpu.CompilerParams(collective_id=1, has_side_effects=True,
                                             vmem_limit_bytes=63 * 1024 * 1024),
        name="transport",
    )(req, slots, req, src_cent, src_mass.reshape(1, -1), tgt_cent, tgt_mass.reshape(1, -1), tgt_pts,
      tgt_cluster.reshape(TB_DEV, 2, 128), src_pts, src_cluster.reshape(16, 128), tgt_cluster.reshape(64, 128))
    cf, cg, ff, fg = pl.pallas_call(
        split_kernel,
        out_shape=(S((8, 128), f32), S((1, 128), f32), S((16, 128), f32), S((64, 128), f32)),
        in_specs=[VMEM], out_specs=(VMEM,) * 4, name="split",
    )(out)
    return cf.reshape(-1), cg.reshape(-1), ff.reshape(-1), fg.reshape(-1)


def solution(mesh):
    both = ("row", "col")
    in_specs = (P(None, "row"), P(None, "col"), P("row"), P("col"), P(None, both), P(None, both), P(both), P(both),
                P(both, None))
    out_specs = (P("row"), P("col"), P(both), P(both))
    return jax.shard_map(on_device, mesh=mesh, in_specs=in_specs, out_specs=out_specs, check_vma=False)
```
